256 devices in a mesh: ta: 4 (over y), gy: 16 (over z, core), gx: 4 (over x).
Axes of the slice: x: 4, y: 4, z: 8, core: 2. Of those that a mesh axis runs over, the one named last changes fastest.
Arguments:
- features: bfloat16 [16, 32, 416, 192], P('ta', 'gy', 'gx'), may hold values from -6 to 6
- gain_first: float32 [192], replicated, may hold values from 0.1 to 1.9
- kernel_first: bfloat16 [3, 3, 3, 192, 192], replicated, may hold values from -0.078125 to 0.078125
- bias_first: float32 [192], replicated, may hold values from -3 to 3
- gain_second: float32 [192], replicated, may hold values from 0.1 to 1.9
- kernel_second: bfloat16 [3, 3, 3, 192, 192], replicated, may hold values from -0.078125 to 0.078125
- bias_second: float32 [192], replicated, may hold values from -3 to 3
Outputs:
- block_out: bfloat16 [16, 32, 416, 192], P('ta', 'gy', 'gx')
The draws below stay inside these ranges and needn't reach their ends.
All inputs are finite; a program needn't handle non-finite values.
Results may differ from the reference program's by a relative error of at most 0.0075.
Values may be sent and summed in bfloat16 or wider, within the bound.
No kernel may reach another device: no remote copies, remote signals or barrier semaphores. Data moves between devices by JAX's collectives and lax.ppermute only.
A program may use at most 64 MiB of HBM per device.

```python
import jax
import jax.numpy as jnp
from jax import lax

C = 192
W = 416
FRAMES = 16
H = 32


def levels(stream_key, dims, split, low, top_value):
    level = 1.0
    for dim, parts in split:
        heights = jax.random.uniform(jax.random.fold_in(jax.random.fold_in(stream_key, 6), dim), (parts,), jnp.float32, low / len(split), top_value / len(split))
        level = level * jnp.repeat(jnp.exp(heights), dims[dim] // parts).reshape((-1,) + (1,) * (len(dims) - 1 - dim))
    return level


def bell_draw(stream_key, dims, spread, bound, cuts=(), kind=jnp.bfloat16):
    factor_of = levels(stream_key, dims, cuts, -0.22, 0.18) if cuts else 1.0
    array = jax.random.normal(stream_key, dims, jnp.float32) * spread * factor_of
    return jnp.minimum(jnp.maximum(array, -bound), bound).astype(kind)


def setup_inputs(seed: int = 0) -> dict:
    streams_of = jax.random.split(jax.random.key(seed), 8)
    features = bell_draw(streams_of[0], (FRAMES, H, W, C), 1.0, 6.0, ((0, 4), (1, 16), (2, 4)))
    gain_first = jnp.clip(1.0 + 0.18 * jax.random.normal(streams_of[1], (C,), jnp.float32), 0.1, 1.9)
    kernel_first = bell_draw(streams_of[2], (3, 3, 3, C, C), (27 * C) ** -0.5, 0.078125)
    bias_first = bell_draw(streams_of[3], (C,), 0.5, 3.0, (), jnp.float32)
    gain_second = jnp.clip(1.0 + 0.18 * jax.random.normal(streams_of[4], (C,), jnp.float32), 0.1, 1.9)
    kernel_second = bell_draw(streams_of[5], (3, 3, 3, C, C), (27 * C) ** -0.5, 0.078125)
    bias_second = bell_draw(streams_of[6], (C,), 0.5, 3.0, (), jnp.float32)
    return dict(features=features, gain_first=gain_first, kernel_first=kernel_first, bias_first=bias_first, gain_second=gain_second, kernel_second=kernel_second, bias_second=bias_second)


epsilon = 1e-06

def activate(field, gain):
    field = field.astype(jnp.float32)
    meansq = lax.optimization_barrier(jnp.mean(field * field, axis=-1, keepdims=True))
    return jax.nn.silu(field * lax.rsqrt(meansq + epsilon) * gain).astype(jnp.bfloat16)

def convolve(source, kernel, bias):
    frames, rows, cols, channels = source.shape
    padded = jnp.pad(source, ((2, 0), (1, 1), (1, 1), (0, 0)))

    def one_frame(index):
        window = lax.dynamic_slice_in_dim(padded, index, 3, 0)
        total = jnp.zeros((rows * cols, kernel.shape[-1]), jnp.float32)
        for delta_t in range(3):
            for delta_y in range(3):
                for delta_x in range(3):
                    piece = window[delta_t, delta_y:delta_y + rows, delta_x:delta_x + cols].reshape(-1, channels)
                    total = total + jnp.dot(piece, kernel[delta_t, delta_y, delta_x], preferred_element_type=jnp.float32)
        return total.reshape(rows, cols, -1) + bias
    return lax.map(one_frame, jnp.arange(frames, dtype=jnp.int32))

def reference(features, gain_first, kernel_first, bias_first, gain_second, kernel_second, bias_second):
    first = activate(features, gain_first)
    middle = convolve(first, kernel_first, bias_first).astype(jnp.bfloat16)
    second = activate(middle, gain_second)
    result = convolve(second, kernel_second, bias_second) + features.astype(jnp.float32)
    return result.astype(jnp.bfloat16)
```

```python
import functools

import jax
import jax.numpy as jnp
from jax import lax
from jax.experimental import pallas as pl
from jax.experimental.pallas import tpu as pltpu
from jax.sharding import PartitionSpec as P


epsilon = 1e-06
axes = ("ta", "gy", "gx")
ROWS, COLS, TILE, CYC, CH, LANE = 2, 104, 8, 112, 192, 128
HI = CH - LANE
TILES = COLS // TILE
VMEM = pl.BlockSpec(memory_space=pltpu.VMEM)
SMEM = pl.BlockSpec(memory_space=pltpu.SMEM)
ANY = pl.BlockSpec(memory_space=pl.ANY)
params = pltpu.CompilerParams(vmem_limit_bytes=56 << 20)


def act(field, gain):
    meansq = jnp.mean(field * field, axis=-1, keepdims=True)
    u = field * lax.rsqrt(meansq + epsilon) * gain
    return u / (1.0 + jnp.exp(-u))


def pack(even, odd):
    high = jnp.concatenate([even[:, LANE:], odd[:, LANE:]], axis=1)
    return even[:, :LANE], odd[:, :LANE], high


def first_kernel(flags, feat, gain, mine, on, cr, edge):
    core = flags[0]
    frames = feat.shape[0]
    for slot in range(ROWS):
        row = jnp.where(core == 0, 1 - slot, slot)
        for f in range(0, frames, 2):
            pair = [act(feat[f + e, row].astype(jnp.float32), gain[...]).astype(jnp.bfloat16) for e in range(2)]
            for k, slab in enumerate(pack(*pair)):
                n = 3 * (f // 2) + k
                mine[slot, n] = slab
                left, right = slab[:TILE], slab[COLS - TILE :]
                edge[slot, n] = jnp.where(core == 0, right, left)
                on[slot_base + slot * 6 + n] = jnp.where(core == 0, left, right)
                if slot == 0:
                    on[n * TILES : (n + 1) * TILES] = slab.reshape(TILES, TILE, LANE)
                else:
                    cr[n * TILES : (n + 1) * TILES] = slab.reshape(TILES, TILE, LANE)


slot_base = 6 * TILES


def weight_copies(kernel, weight, sems, core):
    copies = []
    for q in range(3):
        source = jnp.where(core == 0, 2 - q, q)
        copies.append((kernel.at[:, source, :, :LANE, :], weight.at[:, 4 * q : 4 * q + 3]))
        for r in range(3):
            tile, half = (4 * q + 3, r) if r < 2 else (12 + q // 2, q % 2)
            copies.append(
                (kernel.at[:, source, r, LANE:, :], weight.at[:, tile, HI * half : HI * (half + 1), :])
            )
    return [pltpu.make_async_copy(a, b, sems.at[n]) for n, (a, b) in enumerate(copies)]


def rolled(x, by):
    return jnp.concatenate([x[-by:], x[:-by]], axis=0)


def put_row(taps, row, f, low, high):
    for e in range(2):
        taps[row, f + e, :, 0:128] = rolled(low[e], 1)
        taps[row, f + e, :, 128:256] = low[e]
        taps[row, f + e, :, 256:384] = rolled(low[e], -1)
    before, after = rolled(high, 1), rolled(high, -1)
    for e in range(2):
        half = slice(HI * e, HI * (e + 1))
        taps[row, f + e, :, 384:448] = before[:, half]
        taps[row, f + e, :, 448:512] = high[:, half]
        taps[row, f + e, :, 512:576] = after[:, half]
        if row > 0:
            taps[row - 1, f + e, :, 576:640] = after[:, half]
        if row > 1:
            taps[row, f + e, :, 576:640] = after[:, half]


def conv_row(taps, weight, row, f, count):
    total = None
    for p in range(3):
        span = slice(f + p, f + p + count)
        parts = [(taps[row + q, span, :, :512], weight[p, 4 * q : 4 * q + 4]) for q in range(3)]
        last = jnp.concatenate([taps[row, span, :, 512:], taps[row + 2, span, :, 512:]], axis=-1)
        parts.append((last, weight[p, 12:14]))
        for cells, k in parts:
            term = jnp.dot(
                cells.reshape(count * CYC, -1), k.reshape(-1, CH), preferred_element_type=jnp.float32
            )
            total = term if total is None else total + term
    return total


def middle_kernel(flags, mine, ta, on, on_prev, cr, cr_prev, rim, kernel, bias, gain, on_out, cr_out, taps, weight, sems):
    core = flags[0]
    copies = weight_copies(kernel, weight, sems, core)
    for c in copies:
        c.start()
    weight[:, 13, HI:, :] = jnp.zeros((3, HI, CH), jnp.bfloat16)

    def tiles(ref, n):
        return ref[n * TILES : (n + 1) * TILES].reshape(COLS, LANE)

    for half in range(2):
        for pair in range(2):
            f = 4 * half + 2 * pair
            for row in range(4):
                slabs = []
                for k in range(3):
                    n = 3 * pair + k
                    if row == 0:
                        body = tiles(on if half else on_prev, n)
                        tip = rim[1 - half, 2, n]
                    elif row == 3:
                        body = tiles(cr if half else cr_prev, n)
                        tip = cr_prev[slot_base + (1 - half) * 6 + n]
                    else:
                        body = (mine if half else ta)[row - 1, n]
                        tip = rim[1 - half, row - 1, n]
                    slabs.append(jnp.concatenate([body, tip], axis=0))
                put_row(taps, row, f, slabs[:2], slabs[2])
    for c in copies:
        c.wait()
    col = lax.broadcasted_iota(jnp.int32, (CYC, 1), 0)
    outside = ((col == COLS) & (flags[3] == 1)) | ((col == CYC - 1) & (flags[2] == 1))
    for slot in range(ROWS):
        for f in range(0, 6, 2):
            total = conv_row(taps, weight, slot, f, 2) + bias[...]
            middle = total.astype(jnp.bfloat16).astype(jnp.float32)
            second = act(middle, gain[...])
            pair = []
            for e in range(2):
                drop = outside | (flags[1] == 1) if f == 0 else outside
                pair.append(jnp.where(drop, 0.0, second[e * CYC : (e + 1) * CYC]).astype(jnp.bfloat16))
            for k, slab in enumerate(pack(*pair)):
                (on_out if slot == 0 else cr_out)[3 * (f // 2) + k] = slab


def last_kernel(flags, mine_on, mine_cr, on, cr, feat, kernel, bias, out, taps, weight, sems):
    core = flags[0]
    copies = weight_copies(kernel, weight, sems, core)
    for c in copies:
        c.start()
    weight[:, 13, HI:, :] = jnp.zeros((3, HI, CH), jnp.bfloat16)
    for f in range(0, 6, 2):
        n = 3 * (f // 2)
        for row, ref in enumerate((on, mine_on, mine_cr, cr)):
            put_row(taps, row, f, [ref[n], ref[n + 1]], ref[n + 2])
    for c in copies:
        c.wait()
    for slot in range(ROWS):
        row = jnp.where(core == 0, 1 - slot, slot)
        for f in range(0, 4, 2):
            total = conv_row(taps, weight, slot, f, 2) + bias[...]
            for e in range(2):
                cells = total[e * CYC : e * CYC + COLS] + feat[f + e, row].astype(jnp.float32)
                out[f + e, row] = cells.astype(jnp.bfloat16)


def shape(*dims):
    return jax.ShapeDtypeStruct(dims, jnp.bfloat16)


def conv_scratch(frames):
    return [
        pltpu.VMEM((4, frames, CYC, 640), jnp.bfloat16),
        pltpu.VMEM((3, 14, LANE, CH), jnp.bfloat16),
        pltpu.SemaphoreType.DMA((12,)),
    ]


def routes(sizes, move):
    pairs = []
    for t in range(sizes[0]):
        for y in range(sizes[1]):
            for x in range(sizes[2]):
                to = move(t, y, x)
                if all(0 <= a < n for a, n in zip(to, sizes)):
                    ids = [(i * sizes[1] + j) * sizes[2] + k for i, j, k in ((t, y, x), to)]
                    pairs.append(tuple(ids))
    return pairs


def local(sizes, features, gain_first, kernel_first, bias_first, gain_second, kernel_second, bias_second):
    def send(array, move):
        return lax.ppermute(array, axes, routes(sizes, move))

    def chip(array):
        return send(array, lambda t, y, x: (t, y ^ 1, x))

    def cross(array):
        return send(array, lambda t, y, x: (t, y + 1 if y % 2 else y - 1, x))

    core = lax.axis_index("gy") % 2
    ta_index, gx_index = lax.axis_index("ta"), lax.axis_index("gx")
    flags = jnp.stack([core, ta_index == 0, gx_index == 0, gx_index == sizes[2] - 1]).astype(jnp.int32)
    row = lambda v: v.reshape(1, CH)

    mine, on_row, cr_row, edge = pl.pallas_call(
        first_kernel,
        out_shape=(shape(2, 6, COLS, LANE), shape(slot_base + 12, TILE, LANE), shape(slot_base, TILE, LANE), shape(2, 6, TILE, LANE)),
        in_specs=[SMEM, VMEM, VMEM],
        out_specs=(VMEM,) * 4,
        compiler_params=params,
        name="first",
    )(flags, features, row(gain_first))

    on = chip(on_row)
    ta = send(mine, lambda t, y, x: (t + 1, y, x))
    cr = cross(cr_row)
    edges = jnp.concatenate([edge.reshape(12, TILE, LANE), on[slot_base:]])
    side = send(edges, lambda t, y, x: (t, y, x - 1 if y % 2 else x + 1))
    side_prev = send(edges, lambda t, y, x: (t + 1, y, x - 1 if y % 2 else x + 1))
    sides = jnp.stack([side, side_prev]).reshape(2, 2, 12, TILE, LANE)
    others = chip(sides)[:, ::-1]
    upper = lax.broadcasted_iota(jnp.int32, sides.shape, 3) < TILE // 2
    rim = jnp.where(upper == (core == 0), others, sides).reshape(2, 4, 6, TILE, LANE)
    on_prev = chip(ta[0].reshape(slot_base, TILE, LANE))
    cr_prev = cross(jnp.concatenate([ta[1].reshape(slot_base, TILE, LANE), rim[:, 1].reshape(12, TILE, LANE)]))

    on_second, cr_second = pl.pallas_call(
        middle_kernel,
        out_shape=(shape(9, CYC, LANE), shape(9, CYC, LANE)),
        in_specs=[SMEM] + [VMEM] * 7 + [ANY, VMEM, VMEM],
        out_specs=(VMEM, VMEM),
        scratch_shapes=conv_scratch(8),
        compiler_params=params,
        name="middle",
    )(flags, mine, ta, on, on_prev, cr, cr_prev, rim, kernel_first, row(bias_first), row(gain_second))

    return pl.pallas_call(
        last_kernel,
        out_shape=jax.ShapeDtypeStruct(features.shape, jnp.bfloat16),
        in_specs=[SMEM] + [VMEM] * 5 + [ANY, VMEM],
        out_specs=VMEM,
        scratch_shapes=conv_scratch(6),
        compiler_params=params,
        name="last",
    )(flags, on_second, cr_second, chip(on_second), cross(cr_second), features, kernel_second, row(bias_second))


def solution(mesh):
    sizes = tuple(mesh.shape[a] for a in axes)
    placed = (P("ta", "gy", "gx", None), P(), P(), P(), P(), P(), P())
    return jax.shard_map(
        functools.partial(local, sizes),
        mesh=mesh,
        in_specs=placed,
        out_specs=P("ta", "gy", "gx", None),
        check_vma=False,
    )
```

```python
import functools

import jax
import jax.numpy as jnp
from jax import lax
from jax.experimental import pallas as pl
from jax.experimental.pallas import tpu as pltpu
from jax.sharding import PartitionSpec as P


epsilon = 1e-06
axes = ("ta", "gy", "gx")
ROWS, COLS, TILE, CYC, CH, LANE = 2, 104, 8, 112, 192, 128
HI = CH - LANE
TILES = COLS // TILE
VMEM = pl.BlockSpec(memory_space=pltpu.VMEM)
ANY = pl.BlockSpec(memory_space=pl.ANY)
SLABS = 6 * TILES
params = pltpu.CompilerParams(vmem_limit_bytes=16 << 20)


def silu(u):
    return u / (1.0 + jnp.exp(-u))


def pack(even, odd):
    high = jnp.concatenate([even[:, LANE:], odd[:, LANE:]], axis=1)
    return even[:, :LANE], odd[:, :LANE], high


def core_index():
    return lax.rem(lax.axis_index("gy"), 2)


def row_of(slot, core):
    return jnp.where(core == 0, 1 - slot, slot)


def load_weights(kernel, weight, sems, core):
    copies = []
    for q in range(3):
        source = jnp.where(core == 0, 2 - q, q)
        base = (0, 4, 9)[q]
        copies.append((kernel.at[:, source, :, :LANE, :], weight.at[:, base : base + 3]))
        for r in range(3):
            tile, half = (base + 3, r) if r < 2 else ((8, 0), (8, 1), (13, 0))[q]
            copies.append((kernel.at[:, source, r, LANE:, :], weight.at[:, tile, HI * half : HI * (half + 1), :]))
    copies = [pltpu.make_async_copy(a, b, sems.at[n]) for n, (a, b) in enumerate(copies)]
    for c in copies:
        c.start()
    weight[:, 13, HI:, :] = jnp.zeros((3, HI, CH), jnp.bfloat16)
    return copies


def first_kernel(feat, gain, kernel, mine, on, cr, edge, weight, sems):
    core = core_index()
    copies = load_weights(kernel, weight, sems, core)
    frames = feat.shape[0]
    for slot in range(ROWS):
        row = row_of(slot, core)
        for f in range(0, frames, 2):
            pair = []
            for e in range(2):
                field = feat[f + e, row].astype(jnp.float32)
                meansq = jnp.mean(field * field, axis=0, keepdims=True)
                normed = (field * lax.rsqrt(meansq + epsilon)).T
                pair.append(silu(normed * gain[...]).astype(jnp.bfloat16))
            for k, slab in enumerate(pack(*pair)):
                n = 3 * (f // 2) + k
                mine[slot, n] = slab
                left, right = slab[:TILE], slab[COLS - TILE :]
                edge[slot, n] = jnp.where(core == 0, right, left)
                on[SLABS + slot * 6 + n] = jnp.where(core == 0, left, right)
                (cr if slot else on)[n * TILES : (n + 1) * TILES] = slab.reshape(TILES, TILE, LANE)
    for c in copies:
        c.wait()


def rolled(x, by):
    return jnp.concatenate([x[-by:], x[:-by]], axis=0)


def put_row(taps, row, f, low, high):
    for e in range(2):
        taps[row, f + e, :, 0:128] = rolled(low[e], 1)
        taps[row, f + e, :, 128:256] = low[e]
        taps[row, f + e, :, 256:384] = rolled(low[e], -1)
    before, after = rolled(high, 1), rolled(high, -1)
    for e in range(2):
        half = slice(HI * e, HI * (e + 1))
        taps[row, f + e, :, 384:448] = before[:, half]
        taps[row, f + e, :, 448:512] = high[:, half]
        taps[row, f + e, :, 512:576] = after[:, half]
        if row > 0:
            taps[row - 1, f + e, :, 576:640] = after[:, half]
        if row in (0, 2):
            taps[row, f + e, :, 576:640] = after[:, half]


def matmul(cells, weight):
    cells = cells.reshape(cells.shape[0] * CYC, cells.shape[-1])
    return jnp.dot(cells, weight.reshape(-1, CH), preferred_element_type=jnp.float32)


def taps_total(taps, weight, f, count, part):
    total = None
    for p in range(3):
        span = slice(f + p, f + p + count)
        if part == "all":
            cells = [taps[0, span, :, :512], taps[1, span, :, :512], taps[0, span, :, 512:], taps[2, span]]
            k = weight[p]
        elif part == "near":
            cells = [taps[1, span, :, :512], taps[2, span, :, :512], taps[1, span, :, 512:]]
            k = weight[p, :9]
        else:
            cells = [taps[0, span]]
            k = weight[p, 9:]
        term = matmul(jnp.concatenate(cells, axis=-1), k)
        total = term if total is None else total + term
    return total


def put_second(out, total, f, bias, gain):
    gx = lax.axis_index("gx")
    col = lax.broadcasted_iota(jnp.int32, (CYC, 1), 0)
    drop = ((col == COLS) & (gx == lax.axis_size("gx") - 1)) | ((col == CYC - 1) & (gx == 0))
    if f == 0:
        drop = drop | (lax.axis_index("ta") == 0)
    middle = (total + bias[...]).astype(jnp.bfloat16).astype(jnp.float32)
    meansq = jnp.mean(middle * middle, axis=-1, keepdims=True)
    second = silu(middle * lax.rsqrt(meansq + epsilon) * gain[...])
    pair = [jnp.where(drop, 0.0, second[e * CYC : (e + 1) * CYC]).astype(jnp.bfloat16) for e in range(2)]
    for k, slab in enumerate(pack(*pair)):
        out[3 * (f // 2) + k] = slab


def tiles(ref, n, tip):
    return jnp.concatenate([ref[n * TILES : (n + 1) * TILES].reshape(COLS, LANE), tip], axis=0)


def middle_near(mine, ta, on, on_prev, rim, weight, bias, gain, kernel, out, partial, weight_next, taps, sems):
    copies = load_weights(kernel, weight_next, sems, core_index())
    for half in range(2):
        for pair in range(2):
            for row in range(3):
                slabs = []
                for n in range(3 * pair, 3 * pair + 3):
                    if row == 0:
                        slabs.append(tiles(on if half else on_prev, n, rim[1 - half, 2, n]))
                    else:
                        body = (mine if half else ta)[row - 1, n]
                        slabs.append(jnp.concatenate([body, rim[1 - half, row - 1, n]], axis=0))
                put_row(taps, row, 4 * half + 2 * pair, slabs[:2], slabs[2])
    for f in range(0, 6, 2):
        put_second(out, taps_total(taps, weight, f, 2, "all"), f, bias, gain)
    for f in range(0, 6, 2):
        partial[f * CYC : (f + 2) * CYC] = taps_total(taps, weight, f, 2, "near")
    for c in copies:
        c.wait()


def middle_far(cr, partial, weight, bias, gain, out, taps):
    for half in range(2):
        for pair in range(2):
            slabs = []
            for n in range(3 * pair, 3 * pair + 3):
                tip = cr[2 * SLABS + (1 - half) * 6 + n]
                slabs.append(tiles(cr, n + 6 * (1 - half), tip))
            put_row(taps, 0, 4 * half + 2 * pair, slabs[:2], slabs[2])
    for f in range(0, 6, 2):
        total = partial[f * CYC : (f + 2) * CYC] + taps_total(taps, weight, f, 2, "far")
        put_second(out, total, f, bias, gain)


def put_last(store, total, feat, f, row, bias):
    total = total + bias[...]
    for e in range(2):
        cells = total[e * CYC : (e + 1) * CYC].T[:, :COLS] + feat[f + e, row].astype(jnp.float32)
        store(f + e, cells.astype(jnp.bfloat16))


def last_near(mine_on, mine_cr, on, feat, weight, bias, out, partial, taps):
    for f in range(0, 6, 2):
        n = 3 * (f // 2)
        for row, ref in enumerate((on, mine_on, mine_cr)):
            put_row(taps, row, f, [ref[n], ref[n + 1]], ref[n + 2])

    def store(f, cells):
        out[f] = cells

    for f in range(0, 4, 2):
        put_last(store, taps_total(taps, weight, f, 2, "all"), feat, f, row_of(0, core_index()), bias)
    for f in range(0, 4, 2):
        partial[f * CYC : (f + 2) * CYC] = taps_total(taps, weight, f, 2, "near")


def last_far(cr, partial, near, feat, weight, bias, out, taps):
    core = core_index()
    for f in range(0, 6, 2):
        n = 3 * (f // 2)
        put_row(taps, 0, f, [cr[n], cr[n + 1]], cr[n + 2])
    for f in range(out.shape[0]):
        out[f, row_of(0, core)] = near[f]

    def store(f, cells):
        out[f, row_of(1, core)] = cells

    for f in range(0, 4, 2):
        total = partial[f * CYC : (f + 2) * CYC] + taps_total(taps, weight, f, 2, "far")
        put_last(store, total, feat, f, row_of(1, core), bias)


def held(*dims, dtype=jnp.bfloat16):
    return pltpu.VMEM(dims, dtype)


def call(name, body, ins, outs, taps=None, sems=False):
    scratch = [] if taps is None else [held(*taps, CYC, 640)]
    if sems:
        scratch.append(pltpu.SemaphoreType.DMA((12,)))
    return pl.pallas_call(
        body,
        out_shape=outs,
        in_specs=[ANY if a.ndim == 5 and a.shape[0] == 3 else VMEM for a in ins],
        out_specs=jax.tree.map(lambda _: VMEM, outs),
        scratch_shapes=scratch,
        compiler_params=params,
        name=name,
    )(*ins)


def routes(sizes, move):
    pairs = []
    for t in range(sizes[0]):
        for y in range(sizes[1]):
            for x in range(sizes[2]):
                to = move(t, y, x)
                if all(0 <= a < n for a, n in zip(to, sizes)):
                    ids = [(i * sizes[1] + j) * sizes[2] + k for i, j, k in ((t, y, x), to)]
                    pairs.append(tuple(ids))
    return pairs


def local(sizes, features, gain_first, kernel_first, bias_first, gain_second, kernel_second, bias_second):
    def send(array, move):
        return lax.ppermute(array, axes, routes(sizes, move))

    def chip(array):
        return send(array, lambda t, y, x: (t, y ^ 1, x))

    def cross(array):
        return send(array, lambda t, y, x: (t, y + 1 if y % 2 else y - 1, x))

    row = lambda v: v.reshape(1, CH)
    feat = jnp.swapaxes(features, 2, 3)
    weights = held(3, 14, LANE, CH)
    second = held(9, CYC, LANE)

    mine, on_row, cr_row, edge, weight = call(
        "first",
        first_kernel,
        (feat, row(gain_first), kernel_first),
        (held(2, 6, COLS, LANE), held(SLABS + 12, TILE, LANE), held(SLABS, TILE, LANE), held(2, 6, TILE, LANE), weights),
        sems=True,
    )
    on = chip(on_row)
    ta = send(mine, lambda t, y, x: (t + 1, y, x))
    edges = jnp.concatenate([edge.reshape(12, TILE, LANE), on[SLABS:]])
    side = send(edges, lambda t, y, x: (t, y, x - 1 if y % 2 else x + 1))
    side_prev = send(edges, lambda t, y, x: (t + 1, y, x - 1 if y % 2 else x + 1))
    sides = jnp.stack([side, side_prev]).reshape(2, 2, 12, TILE, LANE)
    others = chip(sides)[:, ::-1]
    upper = lax.broadcasted_iota(jnp.int32, sides.shape, 3) < TILE // 2
    rim = jnp.where(upper == (core_index() == 0), others, sides).reshape(2, 4, 6, TILE, LANE)
    on_prev = chip(ta[0].reshape(SLABS, TILE, LANE))
    cr = cross(jnp.concatenate([cr_row, ta[1].reshape(SLABS, TILE, LANE), rim[:, 1].reshape(12, TILE, LANE)]))

    norms = (row(bias_first), row(gain_second))
    near, partial, weight_next = call(
        "middle_near",
        middle_near,
        (mine, ta, on, on_prev, rim, weight, *norms, kernel_second),
        (second, held(6 * CYC, CH, dtype=jnp.float32), weights),
        taps=(3, 8),
        sems=True,
    )
    far = call("middle_far", middle_far, (cr, partial, weight, *norms), second, taps=(1, 8))

    bias = row(bias_second)
    out_near, partial = call(
        "last_near",
        last_near,
        (near, far, chip(near), feat, weight_next, bias),
        (held(4, CH, COLS), held(4 * CYC, CH, dtype=jnp.float32)),
        taps=(3, 6),
    )
    out = call(
        "last_far",
        last_far,
        (cross(far), partial, out_near, feat, weight_next, bias),
        jax.ShapeDtypeStruct(feat.shape, jnp.bfloat16),
        taps=(1, 6),
    )
    return jnp.swapaxes(out, 2, 3)


def solution(mesh):
    sizes = tuple(mesh.shape[a] for a in axes)
    placed = (P("ta", "gy", "gx", None), P(), P(), P(), P(), P(), P())
    return jax.shard_map(
        functools.partial(local, sizes),
        mesh=mesh,
        in_specs=placed,
        out_specs=P("ta", "gy", "gx", None),
        check_vma=False,
    )
```

```python
import functools

import jax
import jax.numpy as jnp
from jax import lax
from jax.experimental import pallas as pl
from jax.experimental.pallas import tpu as pltpu
from jax.sharding import PartitionSpec as P


epsilon = 1e-06
axes = ("ta", "gy", "gx")
ROWS, COLS, TILE, CYC, CH, LANE = 2, 104, 8, 112, 192, 128
HI = CH - LANE
TILES = COLS // TILE
VMEM = pl.BlockSpec(memory_space=pltpu.VMEM)
HBM = pl.BlockSpec(memory_space=pltpu.HBM)
SLABS = 6 * TILES
params = pltpu.CompilerParams(vmem_limit_bytes=16 << 20)


def silu(u):
    return u / (1.0 + jnp.exp(-u))


def pack(even, odd):
    high = jnp.concatenate([even[:, LANE:], odd[:, LANE:]], axis=1)
    return even[:, :LANE], odd[:, :LANE], high


def core_index():
    return lax.rem(lax.axis_index("gy"), 2)


def row_of(slot, core):
    return jnp.where(core == 0, 1 - slot, slot)


def weight_parts(kernel, weight, core):
    parts = []
    for q in range(3):
        source = jnp.where(core == 0, 2 - q, q)
        base = (0, 4, 9)[q]
        parts.append((kernel.at[:, source, :, :LANE, :], weight.at[:, base : base + 3]))
        for r in range(3):
            tile, half = (base + 3, r) if r < 2 else ((8, 0), (8, 1), (13, 0))[q]
            parts.append((kernel.at[:, source, r, LANE:, :], weight.at[:, tile, HI * half : HI * (half + 1), :]))
    return parts


def fetch(pairs, sems, start=0):
    copies = [pltpu.make_async_copy(a, b, sems.at[start + n]) for n, (a, b) in enumerate(pairs)]
    for c in copies:
        c.start()
    return copies


def first_kernel(feat_in, gain_in, mine, on, cr, edge, feat, gain, sems):
    core = core_index()
    frames = feat.shape[0]
    order = [(row_of(slot, core), f) for slot in range(ROWS) for f in range(frames)]
    copies = fetch([(gain_in, gain)] + [(feat_in.at[f, row], feat.at[f, row]) for row, f in order], sems)
    copies[0].wait()
    for slot in range(ROWS):
        row = row_of(slot, core)
        for f in range(0, frames, 2):
            pair = []
            for e in range(2):
                copies[1 + slot * frames + f + e].wait()
                field = feat[f + e, row].astype(jnp.float32)
                meansq = jnp.mean(field * field, axis=0, keepdims=True)
                normed = (field * lax.rsqrt(meansq + epsilon)).T
                pair.append(silu(normed * gain[...]).astype(jnp.bfloat16))
            for k, slab in enumerate(pack(*pair)):
                n = 3 * (f // 2) + k
                mine[slot, n] = slab
                left, right = slab[:TILE], slab[COLS - TILE :]
                edge[slot * 6 + n] = jnp.where(core == 0, right, left)
                on[SLABS + slot * 6 + n] = jnp.where(core == 0, left, right)
                (cr if slot else on)[n * TILES : (n + 1) * TILES] = slab.reshape(TILES, TILE, LANE)


def rolled(x, by):
    return jnp.concatenate([x[-by:], x[:-by]], axis=0)


def put_row(taps, row, f, low, high):
    for e in range(2):
        taps[row, f + e, :, 0:128] = rolled(low[e], 1)
        taps[row, f + e, :, 128:256] = low[e]
        taps[row, f + e, :, 256:384] = rolled(low[e], -1)
    before, after = rolled(high, 1), rolled(high, -1)
    for e in range(2):
        half = slice(HI * e, HI * (e + 1))
        taps[row, f + e, :, 384:448] = before[:, half]
        taps[row, f + e, :, 448:512] = high[:, half]
        taps[row, f + e, :, 512:576] = after[:, half]
        if row > 0:
            taps[row - 1, f + e, :, 576:640] = after[:, half]
        if row in (0, 2):
            taps[row, f + e, :, 576:640] = after[:, half]


def matmul(cells, weight):
    cells = cells.reshape(cells.shape[0] * CYC, cells.shape[-1])
    return jnp.dot(cells, weight.reshape(-1, CH), preferred_element_type=jnp.float32)


def taps_total(taps, weight, f, count, part):
    total = None
    for p in range(3):
        span = slice(f + p, f + p + count)
        if part == "all":
            cells = [taps[0, span, :, :512], taps[1, span, :, :512], taps[0, span, :, 512:], taps[2, span]]
            k = weight[p]
        elif part == "near":
            cells = [taps[1, span, :, :512], taps[2, span, :, :512], taps[1, span, :, 512:]]
            k = weight[p, :9]
        else:
            cells = [taps[0, span]]
            k = weight[p, 9:]
        term = matmul(jnp.concatenate(cells, axis=-1), k)
        total = term if total is None else total + term
    return total


def put_second(out, total, f, bias, gain):
    gx = lax.axis_index("gx")
    col = lax.broadcasted_iota(jnp.int32, (CYC, 1), 0)
    drop = ((col == COLS) & (gx == lax.axis_size("gx") - 1)) | ((col == CYC - 1) & (gx == 0))
    if f == 0:
        drop = drop | (lax.axis_index("ta") == 0)
    middle = (total + bias[...]).astype(jnp.bfloat16).astype(jnp.float32)
    meansq = jnp.mean(middle * middle, axis=-1, keepdims=True)
    second = silu(middle * lax.rsqrt(meansq + epsilon) * gain[...])
    pair = [jnp.where(drop, 0.0, second[e * CYC : (e + 1) * CYC]).astype(jnp.bfloat16) for e in range(2)]
    for k, slab in enumerate(pack(*pair)):
        out[3 * (f // 2) + k] = slab


def tiles(ref, n, tip):
    return jnp.concatenate([ref[n * TILES : (n + 1) * TILES].reshape(COLS, LANE), tip], axis=0)


def middle_near(
    mine, ta, on, on_prev, rim, kernel, kernel_next, bias_in, gain_in, bias_next_in,
    out, partial, weight, weight_next, bias, gain, bias_next, taps, sems,
):
    core = core_index()
    vectors = [(bias_in, bias), (gain_in, gain), (bias_next_in, bias_next)]
    copies = fetch(weight_parts(kernel, weight, core) + vectors, sems)
    copies_next = fetch(weight_parts(kernel_next, weight_next, core), sems, len(copies))
    for ref in (weight, weight_next):
        ref[:, 13, HI:, :] = jnp.zeros((3, HI, CH), jnp.bfloat16)
    for half in range(2):
        for pair in range(2):
            for row in range(3):
                slabs = []
                for n in range(3 * pair, 3 * pair + 3):
                    if row == 0:
                        slabs.append(tiles(on if half else on_prev, n, rim[1 - half, 2, n]))
                    else:
                        body = (mine if half else ta)[row - 1, n]
                        slabs.append(jnp.concatenate([body, rim[1 - half, row - 1, n]], axis=0))
                put_row(taps, row, 4 * half + 2 * pair, slabs[:2], slabs[2])
    for c in copies:
        c.wait()
    for f in range(0, 6, 2):
        put_second(out, taps_total(taps, weight, f, 2, "all"), f, bias, gain)
    for f in range(0, 6, 2):
        partial[f * CYC : (f + 2) * CYC] = taps_total(taps, weight, f, 2, "near")
    for c in copies_next:
        c.wait()


def middle_far(cr, partial, weight, bias, gain, out, taps):
    for half in range(2):
        for pair in range(2):
            slabs = []
            for n in range(3 * pair, 3 * pair + 3):
                tip = cr[2 * SLABS + (1 - half) * 6 + n]
                slabs.append(tiles(cr, n + 6 * (1 - half), tip))
            put_row(taps, 0, 4 * half + 2 * pair, slabs[:2], slabs[2])
    for f in range(0, 6, 2):
        total = partial[f * CYC : (f + 2) * CYC] + taps_total(taps, weight, f, 2, "far")
        put_second(out, total, f, bias, gain)


def put_last(store, total, feat, f, row, bias):
    total = total + bias[...]
    for e in range(2):
        cells = total[e * CYC : (e + 1) * CYC].T[:, :COLS] + feat[f + e, row].astype(jnp.float32)
        store(f + e, cells.astype(jnp.bfloat16))


def last_near(mine_on, mine_cr, on, feat, weight, bias, out, partial, taps):
    for f in range(0, 6, 2):
        n = 3 * (f // 2)
        for row, ref in enumerate((on, mine_on, mine_cr)):
            put_row(taps, row, f, [ref[n], ref[n + 1]], ref[n + 2])

    def store(f, cells):
        out[f] = cells

    for f in range(0, 4, 2):
        put_last(store, taps_total(taps, weight, f, 2, "all"), feat, f, row_of(0, core_index()), bias)
    for f in range(0, 4, 2):
        partial[f * CYC : (f + 2) * CYC] = taps_total(taps, weight, f, 2, "near")


def last_far(cr, partial, near, feat, weight, bias, out, taps):
    core = core_index()
    for f in range(0, 6, 2):
        n = 3 * (f // 2)
        put_row(taps, 0, f, [cr[n], cr[n + 1]], cr[n + 2])
    for f in range(out.shape[0]):
        out[f, row_of(0, core)] = near[f]

    def store(f, cells):
        out[f, row_of(1, core)] = cells

    for f in range(0, 4, 2):
        total = partial[f * CYC : (f + 2) * CYC] + taps_total(taps, weight, f, 2, "far")
        put_last(store, total, feat, f, row_of(1, core), bias)


def held(*dims, dtype=jnp.bfloat16):
    return pltpu.VMEM(dims, dtype)


def call(name, body, ins, outs, far=(), taps=None, sems=0):
    scratch = [] if taps is None else [held(*taps, CYC, 640)]
    if sems:
        scratch.append(pltpu.SemaphoreType.DMA((sems,)))
    return pl.pallas_call(
        body,
        out_shape=outs,
        in_specs=[VMEM for _ in ins] + [HBM for _ in far],
        out_specs=jax.tree.map(lambda _: VMEM, outs),
        scratch_shapes=scratch,
        compiler_params=params,
        name=name,
    )(*ins, *(pltpu.with_memory_space_constraint(a, pltpu.HBM) for a in far))


def routes(sizes, move):
    pairs = []
    for t in range(sizes[0]):
        for y in range(sizes[1]):
            for x in range(sizes[2]):
                to = move(t, y, x)
                if all(0 <= a < n for a, n in zip(to, sizes)):
                    ids = [(i * sizes[1] + j) * sizes[2] + k for i, j, k in ((t, y, x), to)]
                    pairs.append(tuple(ids))
    return pairs


def local(sizes, features, gain_first, kernel_first, bias_first, gain_second, kernel_second, bias_second):
    def send(array, move):
        return lax.ppermute(array, axes, routes(sizes, move))

    def chip(array):
        return send(array, lambda t, y, x: (t, y ^ 1, x))

    def cross(array):
        return send(array, lambda t, y, x: (t, y + 1 if y % 2 else y - 1, x))

    row = lambda v: v.reshape(1, CH)
    weights = held(3, 14, LANE, CH)
    second = held(9, CYC, LANE)
    vector = held(1, CH, dtype=jnp.float32)
    strip, rims = held(SLABS, TILE, LANE), held(12, TILE, LANE)

    mine, on_row, cr_row, edge, feat, _ = call(
        "first",
        first_kernel,
        (),
        (held(2, 6, COLS, LANE), held(SLABS + 12, TILE, LANE), strip, rims, held(4, 2, CH, COLS), vector),
        far=(jnp.swapaxes(features, 2, 3), row(gain_first)),
        sems=9,
    )
    on = chip(on_row)
    edges = jnp.concatenate([edge, on[SLABS:]])
    ta = send(mine, lambda t, y, x: (t + 1, y, x))
    side = send(edges, lambda t, y, x: (t, y, x - 1 if y % 2 else x + 1))
    side_prev = send(edges, lambda t, y, x: (t + 1, y, x - 1 if y % 2 else x + 1))
    sides = jnp.stack([side, side_prev]).reshape(2, 2, 12, TILE, LANE)
    others = chip(sides)[:, ::-1]
    upper = lax.broadcasted_iota(jnp.int32, sides.shape, 3) < TILE // 2
    rim = jnp.where(upper == (core_index() == 0), others, sides).reshape(2, 4, 6, TILE, LANE)
    on_prev = chip(ta[0].reshape(SLABS, TILE, LANE))
    cr = cross(jnp.concatenate([cr_row, ta[1].reshape(SLABS, TILE, LANE), rim[:, 1].reshape(12, TILE, LANE)]))

    near, partial, weight, weight_next, bias, gain, bias_next = call(
        "middle_near",
        middle_near,
        (mine, ta, on, on_prev, rim),
        (second, held(6 * CYC, CH, dtype=jnp.float32), weights, weights, vector, vector, vector),
        far=(kernel_first, kernel_second, row(bias_first), row(gain_second), row(bias_second)),
        taps=(3, 8),
        sems=27,
    )
    far = call("middle_far", middle_far, (cr, partial, weight, bias, gain), second, taps=(1, 8))
    out_near, partial = call(
        "last_near",
        last_near,
        (near, far, chip(near), feat, weight_next, bias_next),
        (held(4, CH, COLS), held(4 * CYC, CH, dtype=jnp.float32)),
        taps=(3, 6),
    )
    out = call(
        "last_far",
        last_far,
        (cross(far), partial, out_near, feat, weight_next, bias_next),
        jax.ShapeDtypeStruct(feat.shape, jnp.bfloat16),
        taps=(1, 6),
    )
    return jnp.swapaxes(out, 2, 3)


def solution(mesh):
    sizes = tuple(mesh.shape[a] for a in axes)
    placed = (P("ta", "gy", "gx", None), P(), P(), P(), P(), P(), P())
    return jax.shard_map(
        functools.partial(local, sizes),
        mesh=mesh,
        in_specs=placed,
        out_specs=P("ta", "gy", "gx", None),
        check_vma=False,
    )
```

```python
import functools

import jax
import jax.numpy as jnp
from jax import lax
from jax.experimental import pallas as pl
from jax.experimental.pallas import tpu as pltpu
from jax.sharding import PartitionSpec as P


epsilon = 1e-06
axes = ("ta", "gy", "gx")
ROWS, COLS, TILE, CYC, CH, LANE = 2, 104, 8, 112, 192, 128
HI = CH - LANE
TILES = COLS // TILE
VMEM = pl.BlockSpec(memory_space=pltpu.VMEM)
HBM = pl.BlockSpec(memory_space=pltpu.HBM)
SLABS = 6 * TILES
params = pltpu.CompilerParams(vmem_limit_bytes=16 << 20)


def silu(u):
    return u / (1.0 + jnp.exp(-u))


def pack(even, odd):
    high = jnp.concatenate([even[:, LANE:], odd[:, LANE:]], axis=1)
    return even[:, :LANE], odd[:, :LANE], high


def core_index():
    return lax.rem(lax.axis_index("gy"), 2)


def row_of(slot, core):
    return jnp.where(core == 0, 1 - slot, slot)


def weight_parts(kernel, weight, core):
    parts = []
    for q in range(3):
        source = jnp.where(core == 0, 2 - q, q)
        base = (0, 4, 9)[q]
        parts.append((kernel.at[:, source, :, :LANE, :], weight.at[:, base : base + 3]))
        for r in range(3):
            tile, half = (base + 3, r) if r < 2 else ((8, 0), (8, 1), (13, 0))[q]
            parts.append((kernel.at[:, source, r, LANE:, :], weight.at[:, tile, HI * half : HI * (half + 1), :]))
    return parts


def fetch(pairs, sems, start=0):
    copies = [pltpu.make_async_copy(a, b, sems.at[start + n]) for n, (a, b) in enumerate(pairs)]
    for c in copies:
        c.start()
    return copies


def load_kernel(after, kernel, kernel_next, *refs):
    vectors, outs, sems = refs[:3], refs[3:-1], refs[-1]
    copies = fetch(zip(vectors, outs[2:]), sems)
    for n, source in enumerate((kernel, kernel_next)):
        copies += fetch(weight_parts(source, outs[n], core_index()), sems, len(copies))
        outs[n][:, 13, HI:, :] = jnp.zeros((3, HI, CH), jnp.bfloat16)
    for c in copies:
        c.wait()


def first_kernel(feat_in, gain_in, mine, on, cr, edge, feat, gain, sems):
    core = core_index()
    frames = feat.shape[0]
    order = [(row_of(slot, core), f) for slot in range(ROWS) for f in range(frames)]
    copies = fetch([(gain_in, gain)] + [(feat_in.at[f, row], feat.at[f, row]) for row, f in order], sems)
    for c in copies:
        c.wait()
    gains = jnp.broadcast_to(gain[...], (LANE, CH)).T[:, :COLS]
    for slot in range(ROWS):
        row = row_of(slot, core)
        for f in range(0, frames, 2):
            pair = []
            for e in range(2):
                field = feat[f + e, row].astype(jnp.float32)
                meansq = jnp.mean(field * field, axis=0, keepdims=True)
                first = silu(field * lax.rsqrt(meansq + epsilon) * gains)
                pair.append(first.astype(jnp.bfloat16).T)
            for k, slab in enumerate(pack(*pair)):
                n = 3 * (f // 2) + k
                mine[slot, n] = slab
                left, right = slab[:TILE], slab[COLS - TILE :]
                edge[slot * 6 + n] = jnp.where(core == 0, right, left)
                on[SLABS + slot * 6 + n] = jnp.where(core == 0, left, right)
                (cr if slot else on)[n * TILES : (n + 1) * TILES] = slab.reshape(TILES, TILE, LANE)


def rolled(x, by):
    return jnp.concatenate([x[-by:], x[:-by]], axis=0)


def put_row(taps, row, f, low, high):
    for e in range(2):
        taps[row, f + e, :, 0:128] = rolled(low[e], 1)
        taps[row, f + e, :, 128:256] = low[e]
        taps[row, f + e, :, 256:384] = rolled(low[e], -1)
    before, after = rolled(high, 1), rolled(high, -1)
    for e in range(2):
        half = slice(HI * e, HI * (e + 1))
        taps[row, f + e, :, 384:448] = before[:, half]
        taps[row, f + e, :, 448:512] = high[:, half]
        taps[row, f + e, :, 512:576] = after[:, half]
        if row > 0:
            taps[row - 1, f + e, :, 576:640] = after[:, half]
        if row in (0, 2):
            taps[row, f + e, :, 576:640] = after[:, half]


def matmul(cells, weight):
    cells = cells.reshape(cells.shape[0] * CYC, cells.shape[-1])
    return jnp.dot(cells, weight.reshape(-1, CH), preferred_element_type=jnp.float32)


def taps_term(taps, weight, f, count, part, p):
    span = slice(f + p, f + p + count)
    if part == "all":
        cells = [taps[0, span, :, :512], taps[1, span, :, :512], taps[0, span, :, 512:], taps[2, span]]
        k = weight[p]
    elif part == "near":
        cells = [taps[1, span, :, :512], taps[2, span, :, :512], taps[1, span, :, 512:]]
        k = weight[p, :9]
    else:
        cells = [taps[0, span]]
        k = weight[p, 9:]
    return matmul(jnp.concatenate(cells, axis=-1), k)


def taps_total(taps, weight, f, count, part):
    first, *others = [taps_term(taps, weight, f, count, part, p) for p in range(3)]
    return sum(others, first)


def put_second(out, total, f, bias, gain):
    gx = lax.axis_index("gx")
    col = lax.broadcasted_iota(jnp.int32, (CYC, 1), 0)
    drop = ((col == COLS) & (gx == lax.axis_size("gx") - 1)) | ((col == CYC - 1) & (gx == 0))
    if f == 0:
        drop = drop | (lax.axis_index("ta") == 0)
    middle = (total + bias[...]).astype(jnp.bfloat16).astype(jnp.float32)
    meansq = jnp.mean(middle * middle, axis=-1, keepdims=True)
    second = silu(middle * lax.rsqrt(meansq + epsilon) * gain[...])
    pair = [jnp.where(drop, 0.0, second[e * CYC : (e + 1) * CYC]).astype(jnp.bfloat16) for e in range(2)]
    for k, slab in enumerate(pack(*pair)):
        out[3 * (f // 2) + k] = slab


def tiles(ref, n, tip):
    return jnp.concatenate([ref[n * TILES : (n + 1) * TILES].reshape(COLS, LANE), tip], axis=0)


def middle_near(mine, ta, on, on_prev, rim, weight, bias, gain, out, partial, taps):
    for half in range(2):
        for pair in range(2):
            for row in range(3):
                slabs = []
                for n in range(3 * pair, 3 * pair + 3):
                    if row == 0:
                        slabs.append(tiles(on if half else on_prev, n, rim[1 - half, 2, n]))
                    else:
                        body = (mine if half else ta)[row - 1, n]
                        slabs.append(jnp.concatenate([body, rim[1 - half, row - 1, n]], axis=0))
                put_row(taps, row, 4 * half + 2 * pair, slabs[:2], slabs[2])
    for f in range(0, 6, 2):
        put_second(out, taps_total(taps, weight, f, 2, "all"), f, bias, gain)
    for f in range(0, 6, 2):
        partial[f * CYC : (f + 2) * CYC] = taps_total(taps, weight, f, 2, "near")


def middle_far(cr, partial, weight, bias, gain, out, taps):
    for half in range(2):
        for pair in range(2):
            slabs = []
            for n in range(3 * pair, 3 * pair + 3):
                tip = cr[2 * SLABS + (1 - half) * 6 + n]
                slabs.append(tiles(cr, n + 6 * (1 - half), tip))
            put_row(taps, 0, 4 * half + 2 * pair, slabs[:2], slabs[2])
    for f in range(0, 6, 2):
        total = partial[f * CYC : (f + 2) * CYC] + taps_total(taps, weight, f, 2, "far")
        put_second(out, total, f, bias, gain)


def put_last(store, total, feat, f, row, bias):
    total = total + bias[...]
    for e in range(2):
        cells = total[e * CYC : (e + 1) * CYC].T[:, :COLS] + feat[f + e, row].astype(jnp.float32)
        store(f + e, cells.astype(jnp.bfloat16))


def last_near(mine_on, mine_cr, on, feat, weight, bias, out, partial, taps):
    for f in range(0, 6, 2):
        n = 3 * (f // 2)
        for row, ref in enumerate((on, mine_on, mine_cr)):
            put_row(taps, row, f, [ref[n], ref[n + 1]], ref[n + 2])

    def store(f, cells):
        out[f] = cells

    for f in range(0, 4, 2):
        put_last(store, taps_total(taps, weight, f, 2, "all"), feat, f, row_of(0, core_index()), bias)
    for f in range(0, 4, 2):
        partial[f * CYC : (f + 2) * CYC] = taps_total(taps, weight, f, 2, "near")


def last_far(cr, partial, near, feat, weight, bias, out, taps, far, sems):
    row, near_row = row_of(1, core_index()), row_of(0, core_index())
    frames = feat.shape[0]
    copies = fetch([(near.at[f], out.at[f, near_row]) for f in range(frames)], sems)
    for f in range(0, 6, 2):
        n = 3 * (f // 2)
        put_row(taps, 0, f, [cr[n], cr[n + 1]], cr[n + 2])

    def store(f, cells):
        far[f] = cells
        copies.extend(fetch([(far.at[f], out.at[f, row])], sems, frames + f))

    for f in range(0, 4, 2):
        total = partial[f * CYC : (f + 2) * CYC] + taps_total(taps, weight, f, 2, "far")
        put_last(store, total, feat, f, row, bias)
    for c in copies:
        c.wait()


def held(*dims, dtype=jnp.bfloat16):
    return pltpu.VMEM(dims, dtype)


def call(name, body, ins, outs, far=(), taps=None, scratch=(), sems=0, out_spec=VMEM):
    scratch = ([] if taps is None else [held(*taps, CYC, 640)]) + list(scratch)
    if sems:
        scratch.append(pltpu.SemaphoreType.DMA((sems,)))
    return pl.pallas_call(
        body,
        out_shape=outs,
        in_specs=[VMEM for _ in ins] + [HBM for _ in far],
        out_specs=jax.tree.map(lambda _: out_spec, outs),
        scratch_shapes=scratch,
        compiler_params=params,
        name=name,
    )(*ins, *(pltpu.with_memory_space_constraint(a, pltpu.HBM) for a in far))


def routes(sizes, move):
    pairs = []
    for t in range(sizes[0]):
        for y in range(sizes[1]):
            for x in range(sizes[2]):
                to = move(t, y, x)
                if all(0 <= a < n for a, n in zip(to, sizes)):
                    ids = [(i * sizes[1] + j) * sizes[2] + k for i, j, k in ((t, y, x), to)]
                    pairs.append(tuple(ids))
    return pairs


def local(sizes, features, gain_first, kernel_first, bias_first, gain_second, kernel_second, bias_second):
    def send(array, move):
        return lax.ppermute(array, axes, routes(sizes, move))

    def chip(array):
        return send(array, lambda t, y, x: (t, y ^ 1, x))

    def cross(array):
        return send(array, lambda t, y, x: (t, y + 1 if y % 2 else y - 1, x))

    row = lambda v: v.reshape(1, CH)
    weights = held(3, 14, LANE, CH)
    second = held(9, CYC, LANE)
    vector = held(1, CH, dtype=jnp.float32)
    strip, rims = held(SLABS, TILE, LANE), held(12, TILE, LANE)

    mine, on_row, cr_row, edge, feat, _ = call(
        "first",
        first_kernel,
        (),
        (held(2, 6, COLS, LANE), held(SLABS + 12, TILE, LANE), strip, rims, held(4, 2, CH, COLS), vector),
        far=(jnp.swapaxes(features, 2, 3), row(gain_first)),
        sems=9,
    )
    on = chip(on_row)
    edges = jnp.concatenate([edge, on[SLABS:]])
    ta = send(mine, lambda t, y, x: (t + 1, y, x))
    side = send(edges, lambda t, y, x: (t, y, x - 1 if y % 2 else x + 1))
    side_prev = send(edges, lambda t, y, x: (t + 1, y, x - 1 if y % 2 else x + 1))
    held_args = call(
        "load",
        load_kernel,
        (edges,),
        (weights, weights, vector, vector, vector),
        far=(kernel_first, kernel_second, row(bias_first), row(gain_second), row(bias_second)),
        sems=27,
    )
    side, side_prev, *held_args = lax.optimization_barrier((side, side_prev, *held_args))
    weight, weight_next, bias, gain, bias_next = held_args
    sides = jnp.stack([side, side_prev]).reshape(2, 2, 12, TILE, LANE)
    others = chip(sides)[:, ::-1]
    upper = lax.broadcasted_iota(jnp.int32, sides.shape, 3) < TILE // 2
    rim = jnp.where(upper == (core_index() == 0), others, sides).reshape(2, 4, 6, TILE, LANE)
    on_prev = chip(ta[0].reshape(SLABS, TILE, LANE))
    message = jnp.concatenate([cr_row, ta[1].reshape(SLABS, TILE, LANE), rim[:, 1].reshape(12, TILE, LANE)])
    message, on_prev = lax.optimization_barrier((message, on_prev))
    cr = cross(message)

    near, partial = call(
        "middle_near",
        middle_near,
        (mine, ta, on, on_prev, rim, weight, bias, gain),
        (second, held(6 * CYC, CH, dtype=jnp.float32)),
        taps=(3, 8),
    )
    far = call("middle_far", middle_far, (cr, partial, weight, bias, gain), second, taps=(1, 8))
    out_near, partial = call(
        "last_near",
        last_near,
        (near, far, chip(near), feat, weight_next, bias_next),
        (held(4, CH, COLS), held(4 * CYC, CH, dtype=jnp.float32)),
        taps=(3, 6),
    )
    out = call(
        "last_far",
        last_far,
        (cross(far), partial, out_near, feat, weight_next, bias_next),
        jax.ShapeDtypeStruct(feat.shape, jnp.bfloat16),
        taps=(1, 6),
        scratch=[held(4, CH, COLS)],
        sems=8,
        out_spec=HBM,
    )
    return jnp.swapaxes(out, 2, 3)


def solution(mesh):
    sizes = tuple(mesh.shape[a] for a in axes)
    placed = (P("ta", "gy", "gx", None), P(), P(), P(), P(), P(), P())
    return jax.shard_map(
        functools.partial(local, sizes),
        mesh=mesh,
        in_specs=placed,
        out_specs=P("ta", "gy", "gx", None),
        check_vma=False,
    )
```

```python
import functools

import jax
import jax.numpy as jnp
from jax import lax
from jax.experimental import pallas as pl
from jax.experimental.pallas import tpu as pltpu
from jax.sharding import PartitionSpec as P


epsilon = 1e-06
axes = ("ta", "gy", "gx")
ROWS, COLS, TILE, CYC, CH, LANE = 2, 104, 8, 112, 192, 128
HI = CH - LANE
TILES = COLS // TILE
VMEM = pl.BlockSpec(memory_space=pltpu.VMEM)
HBM = pl.BlockSpec(memory_space=pltpu.HBM)
SLABS = 6 * TILES
params = pltpu.CompilerParams(vmem_limit_bytes=16 << 20)


def silu(u):
    return u / (1.0 + jnp.exp(-u))


def pack(even, odd):
    high = jnp.concatenate([even[:, LANE:], odd[:, LANE:]], axis=1)
    return even[:, :LANE], odd[:, :LANE], high


def core_index():
    return lax.rem(lax.axis_index("gy"), 2)


def row_of(slot, core):
    return jnp.where(core == 0, 1 - slot, slot)


def weight_parts(kernel, weight, core):
    parts = []
    for q in range(3):
        source = jnp.where(core == 0, 2 - q, q)
        base = (0, 4, 9)[q]
        parts.append((kernel.at[:, source, :, :LANE, :], weight.at[:, base : base + 3]))
        for r in range(3):
            tile, half = (base + 3, r) if r < 2 else ((8, 0), (8, 1), (13, 0))[q]
            parts.append((kernel.at[:, source, r, LANE:, :], weight.at[:, tile, HI * half : HI * (half + 1), :]))
    return parts


def fetch(pairs, sems, start=0):
    copies = [pltpu.make_async_copy(a, b, sems.at[start + n]) for n, (a, b) in enumerate(pairs)]
    for c in copies:
        c.start()
    return copies


def load_kernel(after, kernel, *refs):
    vectors, (weight, *outs), sems = refs[:3], refs[3:-1], refs[-1]
    copies = fetch(zip(vectors, outs), sems)
    copies += fetch(weight_parts(kernel, weight, core_index()), sems, len(copies))
    weight[:, 13, HI:, :] = jnp.zeros((3, HI, CH), jnp.bfloat16)
    for c in copies:
        c.wait()


def first_kernel(feat_in, gain_in, mine, on, cr, edge, feat, gain, sems):
    core = core_index()
    frames = feat.shape[0]
    order = [(row_of(slot, core), f) for slot in range(ROWS) for f in range(frames)]
    copies = fetch([(gain_in, gain)] + [(feat_in.at[f, row], feat.at[f, row]) for row, f in order], sems)
    for c in copies:
        c.wait()
    gains = jnp.broadcast_to(gain[...], (LANE, CH)).T[:, :COLS]
    for slot in range(ROWS):
        row = row_of(slot, core)
        for f in range(0, frames, 2):
            pair = []
            for e in range(2):
                field = feat[f + e, row].astype(jnp.float32)
                meansq = jnp.mean(field * field, axis=0, keepdims=True)
                first = silu(field * lax.rsqrt(meansq + epsilon) * gains)
                pair.append(first.astype(jnp.bfloat16).T)
            for k, slab in enumerate(pack(*pair)):
                n = 3 * (f // 2) + k
                mine[slot, n] = slab
                left, right = slab[:2], slab[COLS - 2 :]
                for at in (2 * slot, 4 + 2 * slot):
                    edge[n, at : at + 2] = jnp.where(core == 0, right, left)
                    on[SLABS + n, at : at + 2] = jnp.where(core == 0, left, right)
                (cr if slot else on)[n * TILES : (n + 1) * TILES] = slab.reshape(TILES, TILE, LANE)


def rolled(x, by):
    return jnp.concatenate([x[-by:], x[:-by]], axis=0)


def put_row(taps, row, f, low, high):
    for e in range(2):
        taps[row, f + e, :, 0:128] = rolled(low[e], 1)
        taps[row, f + e, :, 128:256] = low[e]
        taps[row, f + e, :, 256:384] = rolled(low[e], -1)
    before, after = rolled(high, 1), rolled(high, -1)
    for e in range(2):
        half = slice(HI * e, HI * (e + 1))
        taps[row, f + e, :, 384:448] = before[:, half]
        taps[row, f + e, :, 448:512] = high[:, half]
        taps[row, f + e, :, 512:576] = after[:, half]
        if row > 0:
            taps[row - 1, f + e, :, 576:640] = after[:, half]
        if row in (0, 2):
            taps[row, f + e, :, 576:640] = after[:, half]


def matmul(cells, weight):
    cells = cells.reshape(cells.shape[0] * CYC, cells.shape[-1])
    return jnp.dot(cells, weight.reshape(-1, CH), preferred_element_type=jnp.float32)


def taps_term(taps, weight, f, count, part, p):
    span = slice(f + p, f + p + count)
    if part == "all":
        cells = [taps[0, span, :, :512], taps[1, span, :, :512], taps[0, span, :, 512:], taps[2, span]]
        k = weight[p]
    elif part == "near":
        cells = [taps[1, span, :, :512], taps[2, span, :, :512], taps[1, span, :, 512:]]
        k = weight[p, :9]
    else:
        cells = [taps[0, span]]
        k = weight[p, 9:]
    return matmul(jnp.concatenate(cells, axis=-1), k)


def taps_total(taps, weight, f, count, part):
    first, *others = [taps_term(taps, weight, f, count, part, p) for p in range(3)]
    return sum(others, first)


def put_second(out, total, f, bias, gain):
    gx = lax.axis_index("gx")
    col = lax.broadcasted_iota(jnp.int32, (CYC, 1), 0)
    drop = ((col == COLS) & (gx == lax.axis_size("gx") - 1)) | ((col == CYC - 1) & (gx == 0))
    if f == 0:
        drop = drop | (lax.axis_index("ta") == 0)
    middle = (total + bias[...]).astype(jnp.bfloat16).astype(jnp.float32)
    meansq = jnp.mean(middle * middle, axis=-1, keepdims=True)
    second = silu(middle * lax.rsqrt(meansq + epsilon) * gain[...])
    pair = [jnp.where(drop, 0.0, second[e * CYC : (e + 1) * CYC]).astype(jnp.bfloat16) for e in range(2)]
    for k, slab in enumerate(pack(*pair)):
        out[3 * (f // 2) + k] = slab


def tip_of(tile, at, left_first):
    a, b = tile[at : at + 2], tile[at + 4 : at + 6]
    left, right = jnp.where(left_first, a, b), jnp.where(left_first, b, a)
    return jnp.concatenate([right, right, left, left], axis=0)


def tiles(ref, n, tip):
    return jnp.concatenate([ref[n * TILES : (n + 1) * TILES].reshape(COLS, LANE), tip], axis=0)


def middle_near(
    mine, ta, on, on_prev, mine_rim, on_rim, weight, bias, gain, kernel, out, partial, weight_next, taps, sems
):
    core = core_index()
    copies = fetch(weight_parts(kernel, weight_next, core), sems)
    weight_next[:, 13, HI:, :] = jnp.zeros((3, HI, CH), jnp.bfloat16)
    for half in range(2):
        for pair in range(2):
            for row in range(3):
                slabs = []
                for n in range(3 * pair, 3 * pair + 3):
                    if row == 0:
                        slabs.append(tiles(on if half else on_prev, n, tip_of(on_rim[1 - half, n], 0, core == 1)))
                    else:
                        body = (mine if half else ta)[row - 1, n]
                        tip = tip_of(mine_rim[1 - half, n], 2 * (row - 1), core == 0)
                        slabs.append(jnp.concatenate([body, tip], axis=0))
                put_row(taps, row, 4 * half + 2 * pair, slabs[:2], slabs[2])
    for f in range(0, 6, 2):
        put_second(out, taps_total(taps, weight, f, 2, "all"), f, bias, gain)
    for f in range(0, 6, 2):
        partial[f * CYC : (f + 2) * CYC] = taps_total(taps, weight, f, 2, "near")
    for c in copies:
        c.wait()


def middle_far(cr, partial, weight, bias, gain, out, taps):
    for half in range(2):
        for pair in range(2):
            slabs = []
            for n in range(3 * pair, 3 * pair + 3):
                tip = tip_of(cr[2 * SLABS + (1 - half) * 6 + n], 2, core_index() == 1)
                slabs.append(tiles(cr, n + 6 * (1 - half), tip))
            put_row(taps, 0, 4 * half + 2 * pair, slabs[:2], slabs[2])
    for f in range(0, 6, 2):
        total = partial[f * CYC : (f + 2) * CYC] + taps_total(taps, weight, f, 2, "far")
        put_second(out, total, f, bias, gain)


def put_last(store, total, feat, f, row, bias):
    total = total + bias[...]
    for e in range(2):
        cells = total[e * CYC : (e + 1) * CYC].T[:, :COLS] + feat[f + e, row].astype(jnp.float32)
        store(f + e, cells.astype(jnp.bfloat16))


def last_near(mine_on, mine_cr, on, feat, weight, bias, out, partial, taps):
    for f in range(0, 6, 2):
        n = 3 * (f // 2)
        for row, ref in enumerate((on, mine_on, mine_cr)):
            put_row(taps, row, f, [ref[n], ref[n + 1]], ref[n + 2])

    def store(f, cells):
        out[f] = cells

    for f in range(0, 4, 2):
        put_last(store, taps_total(taps, weight, f, 2, "all"), feat, f, row_of(0, core_index()), bias)
    for f in range(0, 4, 2):
        partial[f * CYC : (f + 2) * CYC] = taps_total(taps, weight, f, 2, "near")


def last_far(cr, partial, near, feat, weight, bias, out, taps, far, sems):
    row, near_row = row_of(1, core_index()), row_of(0, core_index())
    frames = feat.shape[0]
    copies = fetch([(near.at[f], out.at[f, near_row]) for f in range(frames)], sems)
    for f in range(0, 6, 2):
        n = 3 * (f // 2)
        put_row(taps, 0, f, [cr[n], cr[n + 1]], cr[n + 2])

    def store(f, cells):
        far[f] = cells
        copies.extend(fetch([(far.at[f], out.at[f, row])], sems, frames + f))

    for f in range(0, 4, 2):
        total = partial[f * CYC : (f + 2) * CYC] + taps_total(taps, weight, f, 2, "far")
        put_last(store, total, feat, f, row, bias)
    for c in copies:
        c.wait()


def held(*dims, dtype=jnp.bfloat16):
    return pltpu.VMEM(dims, dtype)


def call(name, body, ins, outs, far=(), taps=None, scratch=(), sems=0, out_spec=VMEM):
    scratch = ([] if taps is None else [held(*taps, CYC, 640)]) + list(scratch)
    if sems:
        scratch.append(pltpu.SemaphoreType.DMA((sems,)))
    return pl.pallas_call(
        body,
        out_shape=outs,
        in_specs=[VMEM for _ in ins] + [HBM for _ in far],
        out_specs=jax.tree.map(lambda _: out_spec, outs),
        scratch_shapes=scratch,
        compiler_params=params,
        name=name,
    )(*ins, *(pltpu.with_memory_space_constraint(a, pltpu.HBM) for a in far))


def routes(sizes, move):
    pairs = []
    for t in range(sizes[0]):
        for y in range(sizes[1]):
            for x in range(sizes[2]):
                to = move(t, y, x)
                if all(0 <= a < n for a, n in zip(to, sizes)):
                    ids = [(i * sizes[1] + j) * sizes[2] + k for i, j, k in ((t, y, x), to)]
                    pairs.append(tuple(ids))
    return pairs


def local(sizes, features, gain_first, kernel_first, bias_first, gain_second, kernel_second, bias_second):
    def send(array, move):
        return lax.ppermute(array, axes, routes(sizes, move))

    def chip(array):
        return send(array, lambda t, y, x: (t, y ^ 1, x))

    def cross(array):
        return send(array, lambda t, y, x: (t, y + 1 if y % 2 else y - 1, x))

    row = lambda v: v.reshape(1, CH)
    weights = held(3, 14, LANE, CH)
    second = held(9, CYC, LANE)
    vector = held(1, CH, dtype=jnp.float32)
    strip, rims = held(SLABS, TILE, LANE), held(6, TILE, LANE)

    mine, on_row, cr_row, edge, feat, _ = call(
        "first",
        first_kernel,
        (),
        (held(2, 6, COLS, LANE), held(SLABS + 6, TILE, LANE), strip, rims, held(4, 2, CH, COLS), vector),
        far=(jnp.swapaxes(features, 2, 3), row(gain_first)),
        sems=9,
    )
    on = chip(on_row)
    upper = lax.broadcasted_iota(jnp.int32, (TILE, LANE), 0) < TILE // 2
    edges = jnp.where(upper, edge, on[SLABS:])
    ta = send(mine, lambda t, y, x: (t + 1, y, x))
    side = send(edges, lambda t, y, x: (t, y, x - 1 if y % 2 else x + 1))
    side_prev = send(edges, lambda t, y, x: (t + 1, y, x - 1 if y % 2 else x + 1))
    held_args = call(
        "load",
        load_kernel,
        (edges,),
        (weights, vector, vector, vector),
        far=(kernel_first, row(bias_first), row(gain_second), row(bias_second)),
        sems=15,
    )
    side, side_prev, *held_args = lax.optimization_barrier((side, side_prev, *held_args))
    weight, bias, gain, bias_next = held_args
    sides = jnp.stack([side, side_prev])
    others = chip(sides)
    mine_rim, on_rim = jnp.where(upper, sides, others), jnp.where(upper, others, sides)
    on_prev = chip(ta[0].reshape(SLABS, TILE, LANE))
    message = jnp.concatenate([cr_row, ta[1].reshape(SLABS, TILE, LANE), mine_rim.reshape(12, TILE, LANE)])
    message, on_prev = lax.optimization_barrier((message, on_prev))
    cr = cross(message)

    near, partial, weight_next = call(
        "middle_near",
        middle_near,
        (mine, ta, on, on_prev, mine_rim, on_rim, weight, bias, gain),
        (second, held(6 * CYC, CH, dtype=jnp.float32), weights),
        far=(kernel_second,),
        taps=(3, 8),
        sems=12,
    )
    far = call("middle_far", middle_far, (cr, partial, weight, bias, gain), second, taps=(1, 8))
    out_near, partial = call(
        "last_near",
        last_near,
        (near, far, chip(near), feat, weight_next, bias_next),
        (held(4, CH, COLS), held(4 * CYC, CH, dtype=jnp.float32)),
        taps=(3, 6),
    )
    out = call(
        "last_far",
        last_far,
        (cross(far), partial, out_near, feat, weight_next, bias_next),
        jax.ShapeDtypeStruct(feat.shape, jnp.bfloat16),
        taps=(1, 6),
        scratch=[held(4, CH, COLS)],
        sems=8,
        out_spec=HBM,
    )
    return jnp.swapaxes(out, 2, 3)


def solution(mesh):
    sizes = tuple(mesh.shape[a] for a in axes)
    placed = (P("ta", "gy", "gx", None), P(), P(), P(), P(), P(), P())
    return jax.shard_map(
        functools.partial(local, sizes),
        mesh=mesh,
        in_specs=placed,
        out_specs=P("ta", "gy", "gx", None),
        check_vma=False,
    )
```

```python
import functools

import jax
import jax.numpy as jnp
from jax import lax
from jax.experimental import pallas as pl
from jax.experimental.pallas import tpu as pltpu
from jax.sharding import PartitionSpec as P


epsilon = 1e-06
axes = ("ta", "gy", "gx")
ROWS, COLS, TILE, CYC, CH, LANE = 2, 104, 8, 112, 192, 128
HI = CH - LANE
TILES = COLS // TILE
VMEM = pl.BlockSpec(memory_space=pltpu.VMEM)
HBM = pl.BlockSpec(memory_space=pltpu.HBM)
SLABS = 6 * TILES
params = pltpu.CompilerParams(vmem_limit_bytes=16 << 20)


def silu(u):
    return u / (1.0 + jnp.exp(-u))


def pack(even, odd):
    high = jnp.concatenate([even[:, LANE:], odd[:, LANE:]], axis=1)
    return even[:, :LANE], odd[:, :LANE], high


def core_index():
    return lax.rem(lax.axis_index("gy"), 2)


def row_of(slot, core):
    return jnp.where(core == 0, 1 - slot, slot)


def weight_parts(kernel, weight, core):
    parts = []
    for q in range(3):
        source = jnp.where(core == 0, 2 - q, q)
        base = (0, 4, 9)[q]
        parts.append((kernel.at[:, source, :, :LANE, :], weight.at[:, base : base + 3]))
        for r in range(3):
            tile, half = (base + 3, r) if r < 2 else ((8, 0), (8, 1), (13, 0))[q]
            parts.append((kernel.at[:, source, r, LANE:, :], weight.at[:, tile, HI * half : HI * (half + 1), :]))
    return parts


def fetch(pairs, sems, start=0):
    copies = [pltpu.make_async_copy(a, b, sems.at[start + n]) for n, (a, b) in enumerate(pairs)]
    for c in copies:
        c.start()
    return copies


def load_kernel(after, kernel, *refs):
    vectors, (weight, *outs), sems = refs[:3], refs[3:-1], refs[-1]
    copies = fetch(zip(vectors, outs), sems)
    copies += fetch(weight_parts(kernel, weight, core_index()), sems, len(copies))
    weight[:, 13, HI:, :] = jnp.zeros((3, HI, CH), jnp.bfloat16)
    for c in copies:
        c.wait()


def first_kernel(feat_in, gain_in, mine, on, cr, edge, feat, gain, sems):
    core = core_index()
    frames = feat.shape[0]
    order = [(row_of(slot, core), f) for slot in range(ROWS) for f in range(frames)]
    copies = fetch([(gain_in, gain)] + [(feat_in.at[f, row], feat.at[f, row]) for row, f in order], sems)
    for c in copies:
        c.wait()
    gains = jnp.broadcast_to(gain[...], (LANE, CH)).T[:, :COLS]
    for slot in range(ROWS):
        row = row_of(slot, core)
        for f in range(0, frames, 2):
            pair = []
            for e in range(2):
                field = feat[f + e, row].astype(jnp.float32)
                meansq = jnp.mean(field * field, axis=0, keepdims=True)
                first = silu(field * lax.rsqrt(meansq + epsilon) * gains)
                pair.append(first.astype(jnp.bfloat16).T)
            for k, slab in enumerate(pack(*pair)):
                n = 3 * (f // 2) + k
                mine[slot, n] = slab
                left, right = slab[:2], slab[COLS - 2 :]
                for at in (2 * slot, 4 + 2 * slot):
                    edge[n, at : at + 2] = jnp.where(core == 0, left, right)
                    on[SLABS + n, at : at + 2] = jnp.where(core == 0, right, left)
                (cr if slot else on)[n * TILES : (n + 1) * TILES] = slab.reshape(TILES, TILE, LANE)


def rolled(x, by):
    return jnp.concatenate([x[-by:], x[:-by]], axis=0)


def put_row(taps, row, f, low, high):
    for e in range(2):
        taps[row, f + e, :, 0:128] = rolled(low[e], 1)
        taps[row, f + e, :, 128:256] = low[e]
        taps[row, f + e, :, 256:384] = rolled(low[e], -1)
    before, after = rolled(high, 1), rolled(high, -1)
    for e in range(2):
        half = slice(HI * e, HI * (e + 1))
        taps[row, f + e, :, 384:448] = before[:, half]
        taps[row, f + e, :, 448:512] = high[:, half]
        taps[row, f + e, :, 512:576] = after[:, half]
        if row > 0:
            taps[row - 1, f + e, :, 576:640] = after[:, half]
        if row in (0, 2):
            taps[row, f + e, :, 576:640] = after[:, half]


def matmul(cells, weight):
    cells = cells.reshape(cells.shape[0] * CYC, cells.shape[-1])
    return jnp.dot(cells, weight.reshape(-1, CH), preferred_element_type=jnp.float32)


def taps_term(taps, weight, f, count, part, p):
    span = slice(f + p, f + p + count)
    if part == "all":
        cells = [taps[0, span, :, :512], taps[1, span, :, :512], taps[0, span, :, 512:], taps[2, span]]
        k = weight[p]
    elif part == "near":
        cells = [taps[1, span, :, :512], taps[2, span, :, :512], taps[1, span, :, 512:]]
        k = weight[p, :9]
    else:
        cells = [taps[0, span]]
        k = weight[p, 9:]
    return matmul(jnp.concatenate(cells, axis=-1), k)


def taps_total(taps, weight, f, count, part):
    first, *others = [taps_term(taps, weight, f, count, part, p) for p in range(3)]
    return sum(others, first)


def put_second(out, total, f, bias, gain):
    gx = lax.axis_index("gx")
    col = lax.broadcasted_iota(jnp.int32, (CYC, 1), 0)
    drop = ((col == COLS) & (gx == lax.axis_size("gx") - 1)) | ((col == CYC - 1) & (gx == 0))
    if f == 0:
        drop = drop | (lax.axis_index("ta") == 0)
    middle = (total + bias[...]).astype(jnp.bfloat16).astype(jnp.float32)
    meansq = jnp.mean(middle * middle, axis=-1, keepdims=True)
    second = silu(middle * lax.rsqrt(meansq + epsilon) * gain[...])
    pair = [jnp.where(drop, 0.0, second[e * CYC : (e + 1) * CYC]).astype(jnp.bfloat16) for e in range(2)]
    for k, slab in enumerate(pack(*pair)):
        out[3 * (f // 2) + k] = slab


def tip_of(tile, at, left_first):
    a, b = tile[at : at + 2], tile[at + 4 : at + 6]
    left, right = jnp.where(left_first, a, b), jnp.where(left_first, b, a)
    return jnp.concatenate([right, right, left, left], axis=0)


def tiles(ref, n, tip):
    return jnp.concatenate([ref[n * TILES : (n + 1) * TILES].reshape(COLS, LANE), tip], axis=0)


def middle_near(
    mine, ta, on, on_prev, mine_rim, on_rim, weight, bias, gain, kernel, out, partial, weight_next, taps, sems
):
    core = core_index()
    copies = fetch(weight_parts(kernel, weight_next, core), sems)
    weight_next[:, 13, HI:, :] = jnp.zeros((3, HI, CH), jnp.bfloat16)
    for half in range(2):
        for pair in range(2):
            for row in range(3):
                slabs = []
                for n in range(3 * pair, 3 * pair + 3):
                    if row == 0:
                        slabs.append(tiles(on if half else on_prev, n, tip_of(on_rim[1 - half, n], 0, core == 0)))
                    else:
                        body = (mine if half else ta)[row - 1, n]
                        tip = tip_of(mine_rim[1 - half, n], 2 * (row - 1), core == 1)
                        slabs.append(jnp.concatenate([body, tip], axis=0))
                put_row(taps, row, 4 * half + 2 * pair, slabs[:2], slabs[2])
    for f in range(0, 6, 2):
        put_second(out, taps_total(taps, weight, f, 2, "all"), f, bias, gain)
    for f in range(0, 6, 2):
        partial[f * CYC : (f + 2) * CYC] = taps_total(taps, weight, f, 2, "near")
    for c in copies:
        c.wait()


def middle_far(cr, partial, weight, bias, gain, out, taps):
    for half in range(2):
        for pair in range(2):
            slabs = []
            for n in range(3 * pair, 3 * pair + 3):
                tip = tip_of(cr[2 * SLABS + (1 - half) * 6 + n], 2, core_index() == 0)
                slabs.append(tiles(cr, n + 6 * (1 - half), tip))
            put_row(taps, 0, 4 * half + 2 * pair, slabs[:2], slabs[2])
    for f in range(0, 6, 2):
        total = partial[f * CYC : (f + 2) * CYC] + taps_total(taps, weight, f, 2, "far")
        put_second(out, total, f, bias, gain)


def put_last(store, total, feat, f, row, bias):
    total = total + bias[...]
    for e in range(2):
        cells = total[e * CYC : (e + 1) * CYC].T[:, :COLS] + feat[f + e, row].astype(jnp.float32)
        store(f + e, cells.astype(jnp.bfloat16))


def last_near(mine_on, mine_cr, on, feat, weight, bias, out, partial, taps):
    for f in range(0, 6, 2):
        n = 3 * (f // 2)
        for row, ref in enumerate((on, mine_on, mine_cr)):
            put_row(taps, row, f, [ref[n], ref[n + 1]], ref[n + 2])

    def store(f, cells):
        out[f] = cells

    for f in range(0, 4, 2):
        put_last(store, taps_total(taps, weight, f, 2, "all"), feat, f, row_of(0, core_index()), bias)
    for f in range(0, 4, 2):
        partial[f * CYC : (f + 2) * CYC] = taps_total(taps, weight, f, 2, "near")


def last_far(cr, partial, near, feat, weight, bias, out, taps, far, sems):
    row, near_row = row_of(1, core_index()), row_of(0, core_index())
    frames = feat.shape[0]
    copies = fetch([(near.at[f], out.at[f, near_row]) for f in range(frames)], sems)
    for f in range(0, 6, 2):
        n = 3 * (f // 2)
        put_row(taps, 0, f, [cr[n], cr[n + 1]], cr[n + 2])

    def store(f, cells):
        far[f] = cells
        copies.extend(fetch([(far.at[f], out.at[f, row])], sems, frames + f))

    for f in range(0, 4, 2):
        total = partial[f * CYC : (f + 2) * CYC] + taps_total(taps, weight, f, 2, "far")
        put_last(store, total, feat, f, row, bias)
    for c in copies:
        c.wait()


def held(*dims, dtype=jnp.bfloat16):
    return pltpu.VMEM(dims, dtype)


def call(name, body, ins, outs, far=(), taps=None, scratch=(), sems=0, out_spec=VMEM):
    scratch = ([] if taps is None else [held(*taps, CYC, 640)]) + list(scratch)
    if sems:
        scratch.append(pltpu.SemaphoreType.DMA((sems,)))
    return pl.pallas_call(
        body,
        out_shape=outs,
        in_specs=[VMEM for _ in ins] + [HBM for _ in far],
        out_specs=jax.tree.map(lambda _: out_spec, outs),
        scratch_shapes=scratch,
        compiler_params=params,
        name=name,
    )(*ins, *(pltpu.with_memory_space_constraint(a, pltpu.HBM) for a in far))


def routes(sizes, move):
    pairs = []
    for t in range(sizes[0]):
        for y in range(sizes[1]):
            for x in range(sizes[2]):
                to = move(t, y, x)
                if all(0 <= a < n for a, n in zip(to, sizes)):
                    ids = [(i * sizes[1] + j) * sizes[2] + k for i, j, k in ((t, y, x), to)]
                    pairs.append(tuple(ids))
    return pairs


def local(sizes, features, gain_first, kernel_first, bias_first, gain_second, kernel_second, bias_second):
    def send(array, move):
        return lax.ppermute(array, axes, routes(sizes, move))

    def chip(array):
        return send(array, lambda t, y, x: (t, y ^ 1, x))

    def cross(array):
        return send(array, lambda t, y, x: (t, y + 1 if y % 2 else y - 1, x))

    row = lambda v: v.reshape(1, CH)
    weights = held(3, 14, LANE, CH)
    second = held(9, CYC, LANE)
    vector = held(1, CH, dtype=jnp.float32)
    strip, rims = held(SLABS, TILE, LANE), held(6, TILE, LANE)

    mine, on_row, cr_row, edge, feat, _ = call(
        "first",
        first_kernel,
        (),
        (held(2, 6, COLS, LANE), held(SLABS + 6, TILE, LANE), strip, rims, held(4, 2, CH, COLS), vector),
        far=(jnp.swapaxes(features, 2, 3), row(gain_first)),
        sems=9,
    )
    on = chip(on_row)
    upper = lax.broadcasted_iota(jnp.int32, (TILE, LANE), 0) < TILE // 2
    edges = jnp.where(upper, edge, on[SLABS:])
    ta = send(mine, lambda t, y, x: (t + 1, y, x))
    side = send(edges, lambda t, y, x: (t, y ^ 1, x + 1 if y % 2 else x - 1))
    side_prev = send(edges, lambda t, y, x: (t + 1, y ^ 1, x + 1 if y % 2 else x - 1))
    held_args = call(
        "load",
        load_kernel,
        (edges,),
        (weights, vector, vector, vector),
        far=(kernel_first, row(bias_first), row(gain_second), row(bias_second)),
        sems=15,
    )
    side, side_prev, *held_args = lax.optimization_barrier((side, side_prev, *held_args))
    weight, bias, gain, bias_next = held_args
    sides = jnp.stack([side, side_prev])
    others = chip(sides)
    mine_rim, on_rim = jnp.where(upper, others, sides), jnp.where(upper, sides, others)
    on_prev = chip(ta[0].reshape(SLABS, TILE, LANE))
    message = jnp.concatenate([cr_row, ta[1].reshape(SLABS, TILE, LANE), mine_rim.reshape(12, TILE, LANE)])
    message, on_prev = lax.optimization_barrier((message, on_prev))
    cr = cross(message)

    near, partial, weight_next = call(
        "middle_near",
        middle_near,
        (mine, ta, on, on_prev, mine_rim, on_rim, weight, bias, gain),
        (second, held(6 * CYC, CH, dtype=jnp.float32), weights),
        far=(kernel_second,),
        taps=(3, 8),
        sems=12,
    )
    far = call("middle_far", middle_far, (cr, partial, weight, bias, gain), second, taps=(1, 8))
    out_near, partial = call(
        "last_near",
        last_near,
        (near, far, chip(near), feat, weight_next, bias_next),
        (held(4, CH, COLS), held(4 * CYC, CH, dtype=jnp.float32)),
        taps=(3, 6),
    )
    out = call(
        "last_far",
        last_far,
        (cross(far), partial, out_near, feat, weight_next, bias_next),
        jax.ShapeDtypeStruct(feat.shape, jnp.bfloat16),
        taps=(1, 6),
        scratch=[held(4, CH, COLS)],
        sems=8,
        out_spec=HBM,
    )
    return jnp.swapaxes(out, 2, 3)


def solution(mesh):
    sizes = tuple(mesh.shape[a] for a in axes)
    placed = (P("ta", "gy", "gx", None), P(), P(), P(), P(), P(), P())
    return jax.shard_map(
        functools.partial(local, sizes),
        mesh=mesh,
        in_specs=placed,
        out_specs=P("ta", "gy", "gx", None),
        check_vma=False,
    )
```

```python
import functools

import jax
import jax.numpy as jnp
from jax import lax
from jax.experimental import pallas as pl
from jax.experimental.pallas import tpu as pltpu
from jax.sharding import PartitionSpec as P


epsilon = 1e-06
axes = ("ta", "gy", "gx")
ROWS, COLS, TILE, CYC, CH, LANE = 2, 104, 8, 112, 192, 128
HI = CH - LANE
TILES = COLS // TILE
VMEM = pl.BlockSpec(memory_space=pltpu.VMEM)
HBM = pl.BlockSpec(memory_space=pltpu.HBM)
SLABS = 6 * TILES
params = pltpu.CompilerParams(vmem_limit_bytes=16 << 20)


def silu(u):
    return u / (1.0 + jnp.exp(-u))


def pack(even, odd):
    high = jnp.concatenate([even[:, LANE:], odd[:, LANE:]], axis=1)
    return even[:, :LANE], odd[:, :LANE], high


def core_index():
    return lax.rem(lax.axis_index("gy"), 2)


def row_of(slot, core):
    return jnp.where(core == 0, 1 - slot, slot)


def weight_parts(kernel, weight, core):
    parts = []
    for q in range(3):
        source = jnp.where(core == 0, 2 - q, q)
        base = (0, 4, 9)[q]
        parts.append((kernel.at[:, source, :, :LANE, :], weight.at[:, base : base + 3]))
        for r in range(3):
            tile, half = (base + 3, r) if r < 2 else ((8, 0), (8, 1), (13, 0))[q]
            parts.append((kernel.at[:, source, r, LANE:, :], weight.at[:, tile, HI * half : HI * (half + 1), :]))
    return parts


def fetch(pairs, sems, start=0):
    copies = [pltpu.make_async_copy(a, b, sems.at[start + n]) for n, (a, b) in enumerate(pairs)]
    for c in copies:
        c.start()
    return copies


def load_kernel(after, kernel, *refs):
    vectors, (weight, *outs), sems = refs[:3], refs[3:-1], refs[-1]
    copies = fetch(zip(vectors, outs), sems)
    copies += fetch(weight_parts(kernel, weight, core_index()), sems, len(copies))
    weight[:, 13, HI:, :] = jnp.zeros((3, HI, CH), jnp.bfloat16)
    for c in copies:
        c.wait()


def first_kernel(feat_in, gain_in, mine, on, cr, edge, feat, gain, sems):
    core = core_index()
    frames = feat.shape[0]
    order = [(row_of(slot, core), f) for slot in range(ROWS) for f in range(frames)]
    copies = fetch([(gain_in, gain)] + [(feat_in.at[f, row], feat.at[f, row]) for row, f in order], sems)
    for c in copies:
        c.wait()
    gains = jnp.broadcast_to(gain[...], (LANE, CH)).T[:, :COLS]
    for slot in range(ROWS):
        row = row_of(slot, core)
        for f in range(0, frames, 2):
            pair = []
            for e in range(2):
                field = feat[f + e, row].astype(jnp.float32)
                meansq = jnp.mean(field * field, axis=0, keepdims=True)
                first = silu(field * lax.rsqrt(meansq + epsilon) * gains)
                pair.append(first.astype(jnp.bfloat16).T)
            for k, slab in enumerate(pack(*pair)):
                n = 3 * (f // 2) + k
                mine[slot, n] = slab
                left, right = slab[:2], slab[COLS - 2 :]
                for at in (2 * slot, 4 + 2 * slot):
                    edge[n, at : at + 2] = jnp.where(core == 0, left, right)
                    on[SLABS + n, at : at + 2] = jnp.where(core == 0, right, left)
                (cr if slot else on)[n * TILES : (n + 1) * TILES] = slab.reshape(TILES, TILE, LANE)


def rolled(x, by):
    return jnp.concatenate([x[-by:], x[:-by]], axis=0)


def put_row(taps, row, f, low, high):
    for e in range(2):
        taps[row, f + e, :, 0:128] = rolled(low[e], 1)
        taps[row, f + e, :, 128:256] = low[e]
        taps[row, f + e, :, 256:384] = rolled(low[e], -1)
    before, after = rolled(high, 1), rolled(high, -1)
    for e in range(2):
        half = slice(HI * e, HI * (e + 1))
        taps[row, f + e, :, 384:448] = before[:, half]
        taps[row, f + e, :, 448:512] = high[:, half]
        taps[row, f + e, :, 512:576] = after[:, half]
        if row > 0:
            taps[row - 1, f + e, :, 576:640] = after[:, half]
        if row in (0, 2):
            taps[row, f + e, :, 576:640] = after[:, half]


def matmul(cells, weight):
    cells = cells.reshape(cells.shape[0] * CYC, cells.shape[-1])
    return jnp.dot(cells, weight.reshape(-1, CH), preferred_element_type=jnp.float32)


def taps_term(taps, weight, f, count, part, p):
    span = slice(f + p, f + p + count)
    if part == "all":
        cells = [taps[0, span, :, :512], taps[1, span, :, :512], taps[0, span, :, 512:], taps[2, span]]
        k = weight[p]
    elif part == "near":
        cells = [taps[1, span, :, :512], taps[2, span, :, :512], taps[1, span, :, 512:]]
        k = weight[p, :9]
    else:
        cells = [taps[0, span]]
        k = weight[p, 9:]
    return matmul(jnp.concatenate(cells, axis=-1), k)


def taps_total(taps, weight, f, count, part):
    first, *others = [taps_term(taps, weight, f, count, part, p) for p in range(3)]
    return sum(others, first)


def put_second(out, total, f, bias, gain):
    gx = lax.axis_index("gx")
    col = lax.broadcasted_iota(jnp.int32, (CYC, 1), 0)
    drop = ((col == COLS) & (gx == lax.axis_size("gx") - 1)) | ((col == CYC - 1) & (gx == 0))
    if f == 0:
        drop = drop | (lax.axis_index("ta") == 0)
    middle = (total + bias[...]).astype(jnp.bfloat16).astype(jnp.float32)
    meansq = jnp.mean(middle * middle, axis=-1, keepdims=True)
    second = silu(middle * lax.rsqrt(meansq + epsilon) * gain[...])
    pair = [jnp.where(drop, 0.0, second[e * CYC : (e + 1) * CYC]).astype(jnp.bfloat16) for e in range(2)]
    for k, slab in enumerate(pack(*pair)):
        out[3 * (f // 2) + k] = slab


def tip_of(tile, at, left_first):
    a, b = tile[at : at + 2], tile[at + 4 : at + 6]
    left, right = jnp.where(left_first, a, b), jnp.where(left_first, b, a)
    return jnp.concatenate([right, right, left, left], axis=0)


def tiles(ref, n, tip):
    return jnp.concatenate([ref[n * TILES : (n + 1) * TILES].reshape(COLS, LANE), tip], axis=0)


def middle_near(
    mine, ta, on, on_prev, mine_rim, on_rim, weight, bias, gain, kernel, out, partial, weight_next, taps, sems
):
    core = core_index()
    copies = fetch(weight_parts(kernel, weight_next, core), sems)
    weight_next[:, 13, HI:, :] = jnp.zeros((3, HI, CH), jnp.bfloat16)
    for half in range(2):
        for pair in range(2):
            for row in range(3):
                slabs = []
                for n in range(3 * pair, 3 * pair + 3):
                    if row == 0:
                        slabs.append(tiles(on if half else on_prev, n, tip_of(on_rim[1 - half, n], 0, core == 0)))
                    else:
                        body = (mine if half else ta)[row - 1, n]
                        tip = tip_of(mine_rim[1 - half, n], 2 * (row - 1), core == 1)
                        slabs.append(jnp.concatenate([body, tip], axis=0))
                put_row(taps, row, 4 * half + 2 * pair, slabs[:2], slabs[2])
    for f in range(0, 6, 2):
        put_second(out, taps_total(taps, weight, f, 2, "all"), f, bias, gain)
    for f in range(0, 6, 2):
        partial[f * CYC : (f + 2) * CYC] = taps_total(taps, weight, f, 2, "near")
    for c in copies:
        c.wait()


def middle_far(cr, partial, weight, bias, gain, out, taps):
    for half in range(2):
        for pair in range(2):
            slabs = []
            for n in range(3 * pair, 3 * pair + 3):
                tip = tip_of(cr[2 * SLABS + (1 - half) * 6 + n], 2, core_index() == 0)
                slabs.append(tiles(cr, n + 6 * (1 - half), tip))
            put_row(taps, 0, 4 * half + 2 * pair, slabs[:2], slabs[2])
    for f in range(0, 6, 2):
        total = partial[f * CYC : (f + 2) * CYC] + taps_total(taps, weight, f, 2, "far")
        put_second(out, total, f, bias, gain)


def put_last(store, total, feat, f, row, bias):
    total = total + bias[...]
    for e in range(2):
        cells = total[e * CYC : (e + 1) * CYC].T[:, :COLS] + feat[f + e, row].astype(jnp.float32)
        store(f + e, cells.astype(jnp.bfloat16))


def last_near(mine_on, mine_cr, on, feat, weight, bias, out, partial, taps):
    for f in range(0, 6, 2):
        n = 3 * (f // 2)
        for row, ref in enumerate((on, mine_on, mine_cr)):
            put_row(taps, row, f, [ref[n], ref[n + 1]], ref[n + 2])

    def store(f, cells):
        out[f] = cells

    for f in range(0, 4, 2):
        put_last(store, taps_total(taps, weight, f, 2, "all"), feat, f, row_of(0, core_index()), bias)
    for f in range(0, 4, 2):
        partial[f * CYC : (f + 2) * CYC] = taps_total(taps, weight, f, 2, "near")


def last_far(cr, partial, near, feat, weight, bias, out, taps, far, sems):
    row, near_row = row_of(1, core_index()), row_of(0, core_index())
    frames = feat.shape[0]
    copies = fetch([(near.at[f], out.at[f, near_row]) for f in range(frames)], sems)
    for f in range(0, 6, 2):
        n = 3 * (f // 2)
        put_row(taps, 0, f, [cr[n], cr[n + 1]], cr[n + 2])

    def store(f, cells):
        far[f] = cells
        copies.extend(fetch([(far.at[f], out.at[f, row])], sems, frames + f))

    for f in range(0, 4, 2):
        total = partial[f * CYC : (f + 2) * CYC] + taps_total(taps, weight, f, 2, "far")
        put_last(store, total, feat, f, row, bias)
    for c in copies:
        c.wait()


def held(*dims, dtype=jnp.bfloat16):
    return pltpu.VMEM(dims, dtype)


def call(name, body, ins, outs, far=(), taps=None, scratch=(), sems=0, out_spec=VMEM):
    scratch = ([] if taps is None else [held(*taps, CYC, 640)]) + list(scratch)
    if sems:
        scratch.append(pltpu.SemaphoreType.DMA((sems,)))
    return pl.pallas_call(
        body,
        out_shape=outs,
        in_specs=[VMEM for _ in ins] + [HBM for _ in far],
        out_specs=jax.tree.map(lambda _: out_spec, outs),
        scratch_shapes=scratch,
        compiler_params=params,
        name=name,
    )(*ins, *(pltpu.with_memory_space_constraint(a, pltpu.HBM) for a in far))


def routes(sizes, move):
    pairs = []
    for t in range(sizes[0]):
        for y in range(sizes[1]):
            for x in range(sizes[2]):
                to = move(t, y, x)
                if all(0 <= a < n for a, n in zip(to, sizes)):
                    ids = [(i * sizes[1] + j) * sizes[2] + k for i, j, k in ((t, y, x), to)]
                    pairs.append(tuple(ids))
    return pairs


def local(sizes, features, gain_first, kernel_first, bias_first, gain_second, kernel_second, bias_second):
    def send(array, move):
        return lax.ppermute(array, axes, routes(sizes, move))

    def chip(array):
        return send(array, lambda t, y, x: (t, y ^ 1, x))

    def cross(array):
        return send(array, lambda t, y, x: (t, y + 1 if y % 2 else y - 1, x))

    row = lambda v: v.reshape(1, CH)
    weights = held(3, 14, LANE, CH)
    second = held(9, CYC, LANE)
    vector = held(1, CH, dtype=jnp.float32)
    strip, rims = held(SLABS, TILE, LANE), held(6, TILE, LANE)

    mine, on_row, cr_row, edge, feat, _ = call(
        "first",
        first_kernel,
        (),
        (held(2, 6, COLS, LANE), held(SLABS + 6, TILE, LANE), strip, rims, held(4, 2, CH, COLS), vector),
        far=(jnp.swapaxes(features, 2, 3), row(gain_first)),
        sems=9,
    )
    on = chip(on_row)
    upper = lax.broadcasted_iota(jnp.int32, (TILE, LANE), 0) < TILE // 2
    edges = jnp.where(upper, edge, on[SLABS:])
    ta = send(mine, lambda t, y, x: (t + 1, y, x))
    side = send(edges, lambda t, y, x: (t, y ^ 1, x + 1 if y % 2 else x - 1))
    side_prev = send(edges, lambda t, y, x: (t + 1, y ^ 1, x + 1 if y % 2 else x - 1))
    held_args = call(
        "load",
        load_kernel,
        (edges,),
        (weights, vector, vector, vector),
        far=(kernel_first, row(bias_first), row(gain_second), row(bias_second)),
        sems=15,
    )
    side, side_prev, *held_args = lax.optimization_barrier((side, side_prev, *held_args))
    weight, bias, gain, bias_next = held_args
    sides = jnp.stack([side, side_prev])
    swapped = chip(jnp.concatenate([ta[0].reshape(SLABS, TILE, LANE), sides.reshape(12, TILE, LANE)]))
    others = swapped[SLABS:].reshape(sides.shape)
    mine_rim, on_rim = jnp.where(upper, others, sides), jnp.where(upper, sides, others)
    message = jnp.concatenate([cr_row, ta[1].reshape(SLABS, TILE, LANE), mine_rim.reshape(12, TILE, LANE)])
    cr = cross(message)

    near, partial, weight_next = call(
        "middle_near",
        middle_near,
        (mine, ta, on, swapped, mine_rim, on_rim, weight, bias, gain),
        (second, held(6 * CYC, CH, dtype=jnp.float32), weights),
        far=(kernel_second,),
        taps=(3, 8),
        sems=12,
    )
    far = call("middle_far", middle_far, (cr, partial, weight, bias, gain), second, taps=(1, 8))
    out_near, partial = call(
        "last_near",
        last_near,
        (near, far, chip(near), feat, weight_next, bias_next),
        (held(4, CH, COLS), held(4 * CYC, CH, dtype=jnp.float32)),
        taps=(3, 6),
    )
    out = call(
        "last_far",
        last_far,
        (cross(far), partial, out_near, feat, weight_next, bias_next),
        jax.ShapeDtypeStruct(feat.shape, jnp.bfloat16),
        taps=(1, 6),
        scratch=[held(4, CH, COLS)],
        sems=8,
        out_spec=HBM,
    )
    return jnp.swapaxes(out, 2, 3)


def solution(mesh):
    sizes = tuple(mesh.shape[a] for a in axes)
    placed = (P("ta", "gy", "gx", None), P(), P(), P(), P(), P(), P())
    return jax.shard_map(
        functools.partial(local, sizes),
        mesh=mesh,
        in_specs=placed,
        out_specs=P("ta", "gy", "gx", None),
        check_vma=False,
    )
```
